128 devices in a mesh: lon: 16 (over y, x), lat: 8 (over z, core).
Axes of the slice: x: 4, y: 4, z: 4, core: 2. Of those that a mesh axis runs over, the one named last changes fastest.
Arguments:
- velocity_start: float32 [2, 1024, 8192], P(None, 'lat', 'lon'), may hold values from -1.5 to 1.5
- forcing: float32 [2, 1024, 8192], P(None, 'lat', 'lon'), may hold values from -1.8 to 1.8
- strength: float32 [1024, 8192], P('lat', 'lon'), may hold values from 1.5 to 3
- mobility: float32 [1024, 8192], P('lat', 'lon'), may hold values from 0.5 to 1
- plan: int32 [8, 64], P('lat', 'lon'), may hold values from -1 to 31, as said below
- stress_in: float32 [8, 32, 3, 128, 128], P('lat', 'lon'), may hold values from -4 to 4
Outputs:
- velocity: float32 [2, 1024, 8192], P(None, 'lat', 'lon')
- force: float32 [2, 1024, 8192], P(None, 'lat', 'lon')
- stress_out: float32 [8, 32, 3, 128, 128], P('lat', 'lon')
The draws below stay inside these ranges and needn't reach their ends.
Inputs may be any that keep to these rules, and one draw needn't show every extreme that they name: plan[r, c] = o * 2 + s puts block (r, c) into slot s of the device at lon index o of the same lat row; -1 marks a block without ice. Every device of a lat row receives exactly 2 blocks, each slot once, and no device sends more than 1 block to one device.
All inputs are finite; a program needn't handle non-finite values.
Results may differ from the reference program's by a relative error of at most 0.00002.
Values sent between devices are 32-bit elements; how exact they have to be, the bound alone decides.
A program may use at most 128 MiB of HBM per device.

```python
import math
import jax
import jax.numpy as jnp

CB = 128
BRD = 1
BCD = 4
NSUB = 4
SLOTS = 2
BROWS = 8
BCOLS = 64
NR = 1024
NC = 8192
N_LON = 16
N_LAT = 8


def draw_plan(key, part):
    per_device = BRD * BCD
    weight = jax.random.randint(jax.random.fold_in(key, 101), (N_LAT, N_LON, 1), 0, 4)
    noise_term = jax.random.randint(jax.random.fold_in(key, 202), (N_LAT, N_LON, per_device), 0, 1000)
    position = jnp.arange(N_LON * per_device, dtype=jnp.int32).reshape(1, N_LON, per_device)
    block_score = ((weight * 1000 + noise_term) * 4096 + position).reshape(N_LAT, N_LON * per_device)
    standing = jnp.argsort(jnp.argsort(-block_score, axis=1), axis=1)
    has_ice = (standing < N_LON * SLOTS).astype(jnp.int32)
    dealt_count = jnp.cumsum(has_ice, axis=1) - has_ice
    row_keys = jax.random.split(jax.random.fold_in(key, 303), N_LAT)
    shuffled = jax.vmap(lambda sub_key: jax.random.permutation(sub_key, N_LON))(row_keys).astype(jnp.int32)
    owner_lon = jnp.take_along_axis(shuffled, dealt_count % N_LON, axis=1)
    plan_rows = jnp.where(has_ice > 0, owner_lon * SLOTS + dealt_count // N_LON, -1)
    plan_grid = plan_rows.reshape(N_LAT, N_LON, BRD, BCD).transpose(0, 2, 1, 3)
    return plan_grid.reshape(N_LAT * BRD, N_LON * BCD).astype(jnp.int32)


def draw_stress_in(key, part):
    full_shape = (N_LAT, N_LON * SLOTS, 3, CB, CB)
    sign_bits = jax.random.randint(jax.random.fold_in(key, 505), (N_LAT, N_LON * SLOTS, 3, 1, 1), 0, 2)
    block_sign = (2 * sign_bits - 1).astype(jnp.float32)
    spread = jax.random.uniform(jax.random.fold_in(key, 606), full_shape, jnp.float32)
    magnitude = 1.5 + 2.5 * spread
    return (block_sign * magnitude).astype(jnp.float32)


def level_of(stream_key, extent, shards, least, top_value):
    level = 1.0
    for dim, parts in shards:
        heights = jax.random.uniform(jax.random.fold_in(jax.random.fold_in(stream_key, 6), dim), (parts,), jnp.float32, least / len(shards), top_value / len(shards))
        level = level * jnp.repeat(jnp.exp(heights), extent[dim] // parts).reshape((-1,) + (1,) * (len(extent) - 1 - dim))
    return level


def scatter_about(rng, extent, scale, limit, shards=(), kind=jnp.bfloat16):
    drawn = jax.random.normal(rng, extent, jnp.float32) * scale
    if len(shards) > 0:
        drawn = level_of(rng, extent, shards, -0.22, 0.18) * drawn
    return jnp.clip(drawn, min=-limit, max=limit).astype(kind)


def setup_inputs(seed: int = 0) -> dict:
    seeds = jax.random.split(jax.random.key(seed), 7)
    return {
        "velocity_start": scatter_about(seeds[0], (2, NR, NC), 0.25, 1.5, ((1, 8), (2, 16)), jnp.float32),
        "forcing": scatter_about(seeds[1], (2, NR, NC), 0.3, 1.8, ((1, 8), (2, 16)), jnp.float32),
        "strength": jnp.clip(jnp.exp(math.log(3.0) - 0.6931472 * jax.random.uniform(seeds[2], (NR, NC), jnp.float32) ** level_of(seeds[2], (NR, NC), ((0, 8), (1, 16)), -0.2, 0.2)), 1.5, 3.0),
        "mobility": jnp.clip(jnp.exp(math.log(1.0) - 0.6931472 * jax.random.uniform(seeds[3], (NR, NC), jnp.float32) ** level_of(seeds[3], (NR, NC), ((0, 8), (1, 16)), -0.2, 0.2)), 0.5, 1.0),
        "plan": draw_plan(jax.random.fold_in(seeds[6], 71), 0),
        "stress_in": draw_stress_in(jax.random.fold_in(seeds[6], 71), 0),
    }


STRESS_DAMPING = 4.0
MOMENTUM_DAMPING = 4.0
ELLIPSE_RATIO = 4.0
FLOOR_SQUARE = 0.0625
OCEAN_DRAG = 1.0
CORIOLIS = 0.3

def interior(array, margin):
    return array[..., margin:array.shape[-2] - margin, margin:array.shape[-1] - margin]

def diff_x(array):
    return (array[..., 1:-1, 2:] - array[..., 1:-1, :-2]) * 0.5

def diff_y(array):
    return (array[..., 2:, 1:-1] - array[..., :-2, 1:-1]) * 0.5

def subcycle(fields, forcing_terms, ice_mask):
    velocity_x, velocity_y, stress_sum, stress_diff, stress_shear = fields
    start_x, start_y, pressure, mobile, push_x, push_y = forcing_terms
    grad_xx = diff_x(velocity_x)
    grad_xy = diff_y(velocity_x)
    grad_yx = diff_x(velocity_y)
    grad_yy = diff_y(velocity_y)
    divergence = grad_xx + grad_yy
    tension = grad_xx - grad_yy
    shearing = grad_xy + grad_yx
    deform_rate = jnp.sqrt(divergence * divergence + (tension * tension + shearing * shearing) / ELLIPSE_RATIO + FLOOR_SQUARE)
    strength_in = interior(pressure, 1)
    mask_in = interior(ice_mask, 1)
    new_sum = mask_in * (STRESS_DAMPING * interior(stress_sum, 1) + strength_in * (divergence / deform_rate - 1.0)) / (1.0 + STRESS_DAMPING)
    new_diff = mask_in * (STRESS_DAMPING * interior(stress_diff, 1) + strength_in * tension / (ELLIPSE_RATIO * deform_rate)) / (1.0 + STRESS_DAMPING)
    new_shear = mask_in * (STRESS_DAMPING * interior(stress_shear, 1) + strength_in * shearing / (2.0 * ELLIPSE_RATIO * deform_rate)) / (1.0 + STRESS_DAMPING)
    mask_core = interior(ice_mask, 2)
    force_x = mask_core * (diff_x(0.5 * (new_sum + new_diff)) + diff_y(new_shear))
    force_y = mask_core * (diff_x(new_shear) + diff_y(0.5 * (new_sum - new_diff)))
    mobile_core = interior(mobile, 2)
    old_x = interior(velocity_x, 2)
    old_y = interior(velocity_y, 2)
    damping = MOMENTUM_DAMPING + 1.0 + mobile_core * OCEAN_DRAG
    next_x = mask_core * (MOMENTUM_DAMPING * old_x + interior(start_x, 2) + mobile_core * (force_x + interior(push_x, 2) + CORIOLIS * old_y)) / damping
    next_y = mask_core * (MOMENTUM_DAMPING * old_y + interior(start_y, 2) + mobile_core * (force_y + interior(push_y, 2) - CORIOLIS * old_x)) / damping
    return ((next_x, next_y, interior(new_sum, 1), interior(new_diff, 1), interior(new_shear, 1)), (force_x, force_y))

def grid_pad(array, margin):
    wrapped = jnp.concatenate([array[..., -margin:], array, array[..., :margin]], axis=-1)
    widths = [(0, 0)] * (wrapped.ndim - 2) + [(margin, margin), (0, 0)]
    return jnp.pad(wrapped, widths)

def reference(velocity_start, forcing, strength, mobility, plan, stress_in):
    activity = (plan >= 0).astype(jnp.float32)
    ice_mask = jnp.repeat(jnp.repeat(activity, CB, axis=0), CB, axis=1)
    flat_stress = stress_in.reshape(N_LAT * N_LON * SLOTS, 3, CB, CB)
    lat_of = (jnp.arange(BROWS, dtype=jnp.int32) // BRD)[:, None]
    gather_index = (lat_of * (N_LON * SLOTS) + jnp.maximum(plan, 0)).reshape(-1).astype(jnp.int32)
    start_blocks = jnp.take(flat_stress, gather_index, axis=0) * activity.reshape(-1)[:, None, None, None]
    stress_grid = start_blocks.reshape(BROWS, BCOLS, 3, CB, CB).transpose(2, 0, 3, 1, 4).reshape(3, BROWS * CB, BCOLS * CB)
    forcing_terms = tuple((grid_pad(item, 2) for item in (velocity_start[0], velocity_start[1], strength, mobility, forcing[0], forcing[1])))
    mask_padded = grid_pad(ice_mask, 2)
    fields = (velocity_start[0] * ice_mask, velocity_start[1] * ice_mask, stress_grid[0], stress_grid[1], stress_grid[2])
    force_pair = None
    for substep in range(NSUB):
        fields, force_pair = subcycle(tuple((grid_pad(item, 2) for item in fields)), forcing_terms, mask_padded)
    velocity = jnp.stack(fields[:2])
    force = jnp.stack(force_pair)
    final_grid = jnp.stack(fields[2:])
    final_blocks = final_grid.reshape(3, BROWS, CB, BCOLS, CB).transpose(1, 3, 0, 2, 4).reshape(BROWS * BCOLS, 3, CB, CB)
    plan_rows = plan.reshape(N_LAT, BRD * BCOLS)
    wanted = jnp.arange(N_LON * SLOTS, dtype=jnp.int32)
    local_index = jnp.argmax(plan_rows[:, None, :] == wanted[None, :, None], axis=-1).astype(jnp.int32)
    block_index = local_index + (jnp.arange(N_LAT, dtype=jnp.int32) * (BRD * BCOLS))[:, None]
    stress_out = jnp.take(final_blocks, block_index.reshape(-1), axis=0).reshape(N_LAT, N_LON * SLOTS, 3, CB, CB)
    return (velocity, force, stress_out)
```

```python
import functools

import jax
import jax.numpy as jnp
from jax import lax
from jax.experimental import pallas as pl
from jax.experimental.pallas import tpu as pltpu
from jax.sharding import PartitionSpec as P

NSUB = 4
LANES = 128
HALO = 8
TOP = 16
MESH = pl.DeviceIdType.MESH


def kernel(
    n_lon, n_lat,
    plan_ref, vel_ref, frc_ref, str_ref, mob_ref, sig_ref,
    o_vel, o_frc, o_sig,
    cst, edge_l, edge_r, halo_r, halo_l,
    plan_own, plan_all, plan_sm, inv_own, inv_sm,
    part, pack, sig, uv, coef, inc, back, home,
    loc_sem, one_sem, p1_s, p1_r, pl_s, pl_r, x_s, x_r, y_s, y_r,
    p2_s, p2_r, h_s, h_r, r1_s, r1_r, r2_s, r2_r,
):
    me = lax.axis_index("lon")
    lat = lax.axis_index("lat")
    right, left = lax.rem(me + 1, n_lon), lax.rem(me + n_lon - 1, n_lon)
    below, above = lax.rem(lat + 1, n_lat), lax.rem(lat + n_lat - 1, n_lat)
    side = LANES
    cols = plan_ref.shape[1]
    slots = sig_ref.shape[1]
    piece = side // n_lon
    tiles = (side + 2 * HALO) // 8
    lane1 = lax.broadcasted_iota(jnp.int32, (1, LANES), 1)
    lane = lax.broadcasted_iota(jnp.int32, (1, 1, LANES), 2)

    def to(src, dst, ss, rs, **where):
        return pltpu.make_async_remote_copy(
            src_ref=src, dst_ref=dst, send_sem=ss, recv_sem=rs,
            device_id=where, device_id_type=MESH,
        )

    def peers(fn):
        def step(k, carry):
            fn(lax.rem(me + k, n_lon))
            return carry
        lax.fori_loop(1, n_lon, step, 0)

    copies = []
    for j in range(cols):
        own = (pl.ds(TOP, side), slice(None))
        src_cols = pl.ds(j * LANES, LANES)
        copies += [
            (vel_ref.at[:, :, src_cols], cst.at[(pl.ds(0, 2), j) + own]),
            (frc_ref.at[:, :, src_cols], cst.at[(pl.ds(2, 2), j) + own]),
            (str_ref.at[:, src_cols], cst.at[(4, j) + own]),
            (mob_ref.at[:, src_cols], cst.at[(5, j) + own]),
        ]
    copies = [pltpu.make_async_copy(s, d, loc_sem.at[i]) for i, (s, d) in enumerate(copies)]
    for c in copies:
        c.start()
    row = jnp.full((1, LANES), -1, jnp.int32)
    for j in range(cols):
        row = jnp.where(lane1 == j, plan_ref[0, j], row)
        active = jnp.where(plan_ref[0, j] >= 0, 1.0, 0.0)
        cst[6, j, pl.ds(TOP, side), :] = jnp.full((side, LANES), active, jnp.float32)
    plan_own[...] = row

    barrier = pltpu.get_barrier_semaphore()
    peers(lambda d: pl.semaphore_signal(barrier, inc=1, device_id={"lon": d}, device_id_type=MESH))
    for other in (above, below):
        pl.semaphore_signal(barrier, inc=1, device_id={"lat": other}, device_id_type=MESH)
    pl.semaphore_wait(barrier, n_lon + 1)

    def stage1(d, sender):
        return to(
            sig_ref.at[0, :, :, pl.ds(d * piece, piece), :],
            part.at[pl.ds(sender * slots, slots)],
            p1_s.at[d], p1_r.at[sender], lon=d,
        )

    def planmsg(d, sender):
        return to(plan_own, plan_all.at[sender], pl_s.at[d], pl_r.at[sender], lon=d)

    peers(lambda d: planmsg(d, me).start())
    peers(lambda d: stage1(d, me).start())
    self1 = pltpu.make_async_copy(
        sig_ref.at[0, :, :, pl.ds(me * piece, piece), :],
        part.at[pl.ds(me * slots, slots)], one_sem.at[0],
    )
    self1.start()
    self_plan = pltpu.make_async_copy(plan_own, plan_all.at[me], one_sem.at[1])
    self_plan.start()

    for c in copies:
        c.wait()
    own_rows = pl.ds(TOP, side)
    pl_left = jnp.zeros((side, LANES), jnp.float32)
    pl_right = jnp.zeros((side, LANES), jnp.float32)
    for f in range(7):
        first, last = cst[f, 0, own_rows, :], cst[f, cols - 1, own_rows, :]
        if f:
            first = pltpu.roll(first, HALO * f, 1)
            last = pltpu.roll(last, LANES - HALO * f, 1)
        pl_left = jnp.where((lane1 >= HALO * f) & (lane1 < HALO * (f + 1)), first, pl_left)
        pl_right = jnp.where(
            (lane1 >= LANES - HALO * (f + 1)) & (lane1 < LANES - HALO * f), last, pl_right
        )
    edge_l[...] = pl_left
    edge_r[...] = pl_right
    x_copies = [
        to(edge_l, halo_r, x_s.at[0], x_r.at[0], lon=left),
        to(edge_r, halo_l, x_s.at[1], x_r.at[1], lon=right),
    ]
    for c in x_copies:
        c.start()
    for c in x_copies:
        c.wait_recv()
    from_r, from_l = halo_r[...], halo_l[...]
    for f in range(7):
        a, b = from_r, from_l
        if f:
            a = pltpu.roll(a, LANES - HALO * f, 1)
            b = pltpu.roll(b, HALO * f, 1)
        cst[f, cols, own_rows, :] = jnp.where(
            lane1 < HALO, a, jnp.where(lane1 >= LANES - HALO, b, 0.0)
        )
    y_copies = [
        to(cst.at[:, :, pl.ds(TOP, HALO), :], cst.at[:, :, pl.ds(TOP + side, HALO), :],
           y_s.at[0], y_r.at[0], lat=above),
        to(cst.at[:, :, pl.ds(TOP + side - HALO, HALO), :], cst.at[:, :, pl.ds(TOP - HALO, HALO), :],
           y_s.at[1], y_r.at[1], lat=below),
    ]
    for c in y_copies:
        c.start()

    peers(lambda d: planmsg(d, d).wait_recv())
    self_plan.wait()
    plan_copy = pltpu.make_async_copy(plan_all, plan_sm, one_sem.at[2])
    plan_copy.start()
    plan_copy.wait()

    peers(lambda d: stage1(d, d).wait_recv())
    self1.wait()

    def seat(d, j):
        return part[jnp.maximum(plan_sm[d, 0, j], 0)]

    def fill(d):
        for j in range(cols):
            pack[d, :, j] = seat(d, j)
        pack[d, :, cols] = jnp.where(
            lane < LANES // 2,
            seat(lax.rem(d + 1, n_lon), 0),
            seat(lax.rem(d + n_lon - 1, n_lon), cols - 1),
        )

    def stage2(d, sender):
        return to(
            pack.at[d], sig.at[:, :, pl.ds(TOP + sender * piece, piece), :],
            p2_s.at[d], p2_r.at[sender], lon=d,
        )

    def send2(d):
        fill(d)
        stage2(d, me).start()

    peers(send2)
    fill(me)
    self2 = pltpu.make_async_copy(
        pack.at[me], sig.at[:, :, pl.ds(TOP + me * piece, piece), :], one_sem.at[3]
    )
    self2.start()

    def invert(d, inv):
        for j in range(cols):
            inv = jnp.where(lane1 == plan_sm[d, 0, j], d * cols + j, inv)
        return inv
    inv_own[...] = lax.fori_loop(0, n_lon, invert, jnp.zeros((1, LANES), jnp.int32))
    inv_copy = pltpu.make_async_copy(inv_own, inv_sm, one_sem.at[4])
    inv_copy.start()

    for c in y_copies:
        c.wait_recv()

    def prepare(t, carry):
        rows = pl.ds(pl.multiple_of(HALO + 8 * t, 8), 8)
        outside = ((t == 0) & (lat == 0)) | ((t == tiles - 1) & (lat == n_lat - 1))
        mask = cst[6, :, rows, :] * jnp.where(outside, 0.0, 1.0)
        mob = cst[5, :, rows, :]
        ratio = mask / (5.0 + mob)
        push = ratio * mob
        sx, sy = cst[0, :, rows, :], cst[1, :, rows, :]
        uv[0, :, rows, :] = mask * sx
        uv[1, :, rows, :] = mask * sy
        coef[0, :, rows, :] = 0.2 * mask * cst[4, :, rows, :]
        coef[1, :, rows, :] = 4.0 * ratio
        coef[2, :, rows, :] = push
        coef[3, :, rows, :] = ratio * sx + push * cst[2, :, rows, :]
        coef[4, :, rows, :] = ratio * sy + push * cst[3, :, rows, :]
        coef[5, :, rows, :] = mask
        return carry

    lax.fori_loop(0, tiles, prepare, 0)

    def east(x):
        r = pltpu.roll(x, LANES - 1, 2)
        return jnp.where(lane == LANES - 1, jnp.concatenate([r[1:], r[:1]], 0), r)

    def west(x):
        r = pltpu.roll(x, 1, 2)
        return jnp.where(lane == 0, jnp.concatenate([r[-1:], r[:-1]], 0), r)

    def diff_x(x):
        return east(x) - west(x)

    def diff_y(ref, f, base):
        return ref[f, :, pl.ds(base + 1, 8), :] - ref[f, :, pl.ds(base - 1, 8), :]

    def increments(base, rows):
        u, v = uv[0, :, rows, :], uv[1, :, rows, :]
        ux, vx = diff_x(u), diff_x(v)
        uy, vy = diff_y(uv, 0, base), diff_y(uv, 1, base)
        div, ten, shr = ux + vy, ux - vy, uy + vx
        a = coef[0, :, rows, :]
        ar = a * lax.rsqrt(div * div + 0.25 * (ten * ten + shr * shr) + 0.25)
        ten4 = 0.25 * ten
        return ar * (div + ten4) - a, ar * (div - ten4) - a, ar * (0.25 * shr)

    def loop(lo, hi, fn):
        def step(t, carry):
            base = pl.multiple_of(HALO + 8 * t, 8)
            fn(base, pl.ds(base, 8))
            return carry
        lax.fori_loop(lo, hi, step, 0)

    def first_increments(base, rows):
        for f, value in enumerate(increments(base, rows)):
            inc[f, :, rows, :] = value

    loop(0, tiles, first_increments)

    def arrived2(sender):
        stage2(sender, sender).wait_recv()

    for sender in range(n_lon):
        @pl.when(me != sender)
        def _(sender=sender):
            arrived2(sender)

        @pl.when(me == sender)
        def _():
            self2.wait()

        if sender == 0:
            up = to(sig.at[:, :, pl.ds(TOP, HALO), :], sig.at[:, :, pl.ds(TOP + side, HALO), :],
                    h_s.at[0], h_r.at[0], lat=above)
            up.start()
    down = to(sig.at[:, :, pl.ds(TOP + side - HALO, HALO), :], sig.at[:, :, pl.ds(TOP - HALO, HALO), :],
              h_s.at[1], h_r.at[1], lat=below)
    down.start()
    for c in (up, down):
        c.wait()

    def stress_first(base, rows):
        w = 0.8 * coef[5, :, rows, :]
        s1, s2, s3 = (sig[f, :, rows, :] for f in range(3))
        sig[0, :, rows, :] = w * (s1 + s2) + inc[0, :, rows, :]
        sig[1, :, rows, :] = w * (s1 - s2) + inc[1, :, rows, :]
        sig[2, :, rows, :] = (w + w) * s3 + inc[2, :, rows, :]

    def stress_next(base, rows):
        for f, value in enumerate(increments(base, rows)):
            sig[f, :, rows, :] = 0.8 * sig[f, :, rows, :] + value

    def momentum(base, rows, emit):
        fx = 0.25 * (diff_x(sig[0, :, rows, :]) + diff_y(sig, 2, base))
        fy = 0.25 * (diff_x(sig[2, :, rows, :]) + diff_y(sig, 1, base))
        u, v = uv[0, :, rows, :], uv[1, :, rows, :]
        keep, push = coef[1, :, rows, :], coef[2, :, rows, :]
        un = keep * u + coef[3, :, rows, :] + push * (fx + 0.3 * v)
        vn = keep * v + coef[4, :, rows, :] + push * (fy - 0.3 * u)
        if not emit:
            uv[0, :, rows, :] = un
            uv[1, :, rows, :] = vn
            return
        mask = coef[5, :, rows, :]
        fx, fy = mask * fx, mask * fy
        out_rows = pl.ds(pl.multiple_of(base - TOP, 8), 8)
        for j in range(cols):
            at = pl.ds(j * LANES, LANES)
            o_vel[0, out_rows, at] = un[j]
            o_vel[1, out_rows, at] = vn[j]
            o_frc[0, out_rows, at] = fx[j]
            o_frc[1, out_rows, at] = fy[j]

    loop(0, tiles, stress_first)

    def subcycle(i, carry):
        loop(0, tiles, functools.partial(momentum, emit=False))
        loop(0, tiles, stress_next)
        return carry

    lax.fori_loop(0, NSUB - 1, subcycle, 0)

    def back1(d, sender):
        return to(
            sig.at[:, pl.ds(0, cols), pl.ds(TOP + d * piece, piece), :], back.at[sender],
            r1_s.at[d], r1_r.at[sender], lon=d,
        )

    peers(lambda d: back1(d, me).start())
    self3 = pltpu.make_async_copy(
        sig.at[:, pl.ds(0, cols), pl.ds(TOP + me * piece, piece), :], back.at[me], one_sem.at[5]
    )
    self3.start()
    loop(1, tiles - 1, functools.partial(momentum, emit=True))

    inv_copy.wait()
    peers(lambda d: back1(d, d).wait_recv())
    self3.wait()

    def refill(d):
        for s in range(slots):
            block = inv_sm[0, d * slots + s]
            got = back[lax.div(block, cols), :, lax.rem(block, cols)]
            home[d, s, 0] = 0.5 * (got[0] + got[1])
            home[d, s, 1] = 0.5 * (got[0] - got[1])
            home[d, s, 2] = 0.5 * got[2]

    def back2(d, sender):
        return to(
            home.at[d], o_sig.at[0, :, :, pl.ds(sender * piece, piece), :],
            r2_s.at[d], r2_r.at[sender], lon=d,
        )

    def send_back2(d):
        refill(d)
        back2(d, me).start()

    peers(send_back2)
    refill(me)
    self4 = pltpu.make_async_copy(
        home.at[me], o_sig.at[0, :, :, pl.ds(me * piece, piece), :], one_sem.at[6]
    )
    self4.start()
    self4.wait()
    peers(lambda d: back2(d, d).wait_recv())

    for c in x_copies + y_copies:
        c.wait_send()

    def drain(d):
        for make in (planmsg, stage1, stage2, back1, back2):
            make(d, me).wait_send()

    peers(drain)


def solution(mesh):
    n_lon, n_lat = mesh.shape["lon"], mesh.shape["lat"]

    def body(velocity_start, forcing, strength, mobility, plan, stress_in):
        cols, slots, side = plan.shape[1], stress_in.shape[1], stress_in.shape[-1]
        piece, wide, tall = side // n_lon, cols + 1, side + 32
        f32, i32 = jnp.float32, jnp.int32
        vmem, dma = pltpu.VMEM, pltpu.SemaphoreType.DMA
        anywhere = pl.BlockSpec(memory_space=pl.ANY)
        inside = pl.BlockSpec(memory_space=pltpu.VMEM)
        return tuple(pl.pallas_call(
            functools.partial(kernel, n_lon, n_lat),
            out_shape=(
                jax.ShapeDtypeStruct(velocity_start.shape, f32),
                jax.ShapeDtypeStruct(forcing.shape, f32),
                jax.ShapeDtypeStruct(stress_in.shape, f32),
            ),
            in_specs=[pl.BlockSpec(memory_space=pltpu.SMEM)] + [anywhere] * 5,
            out_specs=(inside, inside, inside),
            scratch_shapes=[
                vmem((7, wide, tall, LANES), f32),
                vmem((side, LANES), f32),
                vmem((side, LANES), f32),
                vmem((side, LANES), f32),
                vmem((side, LANES), f32),
                vmem((1, LANES), i32),
                vmem((n_lon, 1, LANES), i32),
                pltpu.SMEM((n_lon, 1, LANES), i32),
                vmem((1, LANES), i32),
                pltpu.SMEM((1, LANES), i32),
                vmem((n_lon * slots, 3, piece, LANES), f32),
                vmem((n_lon, 3, wide, piece, LANES), f32),
                vmem((3, wide, tall, LANES), f32),
                vmem((2, wide, tall, LANES), f32),
                vmem((6, wide, tall, LANES), f32),
                vmem((3, wide, tall, LANES), f32),
                vmem((n_lon, 3, cols, piece, LANES), f32),
                vmem((n_lon, slots, 3, piece, LANES), f32),
                dma((4 * cols,)),
                dma((7,)),
                dma((n_lon,)), dma((n_lon,)),
                dma((n_lon,)), dma((n_lon,)),
                dma((2,)), dma((2,)),
                dma((2,)), dma((2,)),
                dma((n_lon,)), dma((n_lon,)),
                dma((2,)), dma((2,)),
                dma((n_lon,)), dma((n_lon,)),
                dma((n_lon,)), dma((n_lon,)),
            ],
            compiler_params=pltpu.CompilerParams(collective_id=0, has_side_effects=True),
        )(plan, velocity_start, forcing, strength, mobility, stress_in))

    placed = (
        P(None, "lat", "lon"),
        P(None, "lat", "lon"),
        P("lat", "lon"),
        P("lat", "lon"),
        P("lat", "lon"),
        P("lat", "lon", None, None, None),
    )
    return jax.shard_map(
        body,
        mesh=mesh,
        in_specs=placed,
        out_specs=(P(None, "lat", "lon"), P(None, "lat", "lon"), P("lat", "lon", None, None, None)),
        check_vma=False,
    )
```

```python
import functools

import jax
import jax.numpy as jnp
from jax import lax
from jax.experimental import pallas as pl
from jax.experimental.pallas import tpu as pltpu
from jax.sharding import PartitionSpec as P

NSUB = 4
PARTS = 2
STRIDE = 7
UNROLL = 3
LANES = 128
HALO = 8
TOP = 16
MESH = pl.DeviceIdType.MESH


def kernel(
    n_lon, n_lat,
    plan_ref, vel_ref, frc_ref, str_ref, mob_ref, sig_ref,
    o_vel, o_frc, o_sig,
    cst, edge_l, edge_r, halo_r, halo_l,
    plan_own, plan_all, plan_sm, inv_own, inv_sm,
    part, pack, sig, uv, coef, inc, back, home,
    loc_sem, one_sem, self_sem, p1_s, p1_r, pl_s, pl_r, x_s, x_r, y_s, y_r,
    p2_s, p2_r, h_s, h_r, r1_s, r1_r, r2_s, r2_r,
):
    me = lax.axis_index("lon")
    lat = lax.axis_index("lat")
    right, left = lax.rem(me + 1, n_lon), lax.rem(me + n_lon - 1, n_lon)
    below, above = lax.rem(lat + 1, n_lat), lax.rem(lat + n_lat - 1, n_lat)
    side = LANES
    all_cols = plan_ref.shape[1]
    cols = all_cols // PARTS
    slots = sig_ref.shape[1]
    piece = side // n_lon
    tiles = (side + 2 * HALO) // 8
    lane1 = lax.broadcasted_iota(jnp.int32, (1, LANES), 1)
    lane = lax.broadcasted_iota(jnp.int32, (1, 1, LANES), 2)

    def to(src, dst, ss, rs, **where):
        return pltpu.make_async_remote_copy(
            src_ref=src, dst_ref=dst, send_sem=ss, recv_sem=rs,
            device_id=where, device_id_type=MESH,
        )

    def peers(fn):
        def step(k, carry):
            fn(lax.rem(me + k * STRIDE, n_lon))
            return carry
        lax.fori_loop(1, n_lon, step, 0)

    def rows_of(d):
        return pl.ds(TOP + d * piece, piece)

    barrier = pltpu.get_barrier_semaphore()
    peers(lambda d: pl.semaphore_signal(barrier, inc=1, device_id={"lon": d}, device_id_type=MESH))
    for other in (above, below):
        pl.semaphore_signal(barrier, inc=1, device_id={"lat": other}, device_id_type=MESH)

    own_rows = pl.ds(TOP, side)
    copies = []
    for j in range(all_cols):
        h, t = divmod(j, cols)
        src_cols = pl.ds(j * LANES, LANES)
        copies += [
            (vel_ref.at[:, :, src_cols], cst.at[h, pl.ds(0, 2), t, own_rows, :]),
            (frc_ref.at[:, :, src_cols], cst.at[h, pl.ds(2, 2), t, own_rows, :]),
            (str_ref.at[:, src_cols], cst.at[h, 4, t, own_rows, :]),
            (mob_ref.at[:, src_cols], cst.at[h, 5, t, own_rows, :]),
        ]
    copies = [pltpu.make_async_copy(s, d, loc_sem.at[i]) for i, (s, d) in enumerate(copies)]
    for c in copies:
        c.start()
    row = jnp.full((1, LANES), -1, jnp.int32)
    for j in range(all_cols):
        h, t = divmod(j, cols)
        row = jnp.where(lane1 == j, plan_ref[0, j], row)
        active = jnp.where(plan_ref[0, j] >= 0, 1.0, 0.0)
        cst[h, 6, t, own_rows, :] = jnp.full((side, LANES), active, jnp.float32)
    plan_own[...] = row
    for c in copies:
        c.wait()

    to_left = jnp.zeros((side, LANES), jnp.float32)
    to_right = jnp.zeros((side, LANES), jnp.float32)
    for f in range(7):
        first, last = cst[0, f, 0, own_rows, :], cst[PARTS - 1, f, cols - 1, own_rows, :]
        if f:
            first = pltpu.roll(first, HALO * f, 1)
            last = pltpu.roll(last, LANES - HALO * f, 1)
        to_left = jnp.where((lane1 >= HALO * f) & (lane1 < HALO * (f + 1)), first, to_left)
        to_right = jnp.where(
            (lane1 >= LANES - HALO * (f + 1)) & (lane1 < LANES - HALO * f), last, to_right
        )
    edge_l[...] = to_left
    edge_r[...] = to_right
    pl.semaphore_wait(barrier, n_lon + 1)

    def stage1(d, sender):
        return to(
            sig_ref.at[0, :, :, pl.ds(d * piece, piece), :],
            part.at[pl.ds(sender * slots, slots)],
            p1_s.at[d], p1_r.at[sender], lon=d,
        )

    def planmsg(d, sender):
        return to(plan_own, plan_all.at[sender], pl_s.at[d], pl_r.at[sender], lon=d)

    x_copies = [
        to(edge_l, halo_r, x_s.at[0], x_r.at[0], lon=left),
        to(edge_r, halo_l, x_s.at[1], x_r.at[1], lon=right),
    ]
    for c in x_copies:
        c.start()
    peers(lambda d: planmsg(d, me).start())
    peers(lambda d: stage1(d, me).start())
    self1 = pltpu.make_async_copy(
        sig_ref.at[0, :, :, pl.ds(me * piece, piece), :],
        part.at[pl.ds(me * slots, slots)], one_sem.at[0],
    )
    self1.start()
    self_plan = pltpu.make_async_copy(plan_own, plan_all.at[me], one_sem.at[1])
    self_plan.start()

    for c in x_copies:
        c.wait_recv()
    for f in range(7):
        from_r, from_l = halo_r[...], halo_l[...]
        if f:
            from_r = pltpu.roll(from_r, LANES - HALO * f, 1)
            from_l = pltpu.roll(from_l, HALO * f, 1)
        for h in range(PARTS):
            a = from_r if h == PARTS - 1 else cst[h + 1, f, 0, own_rows, :]
            b = from_l if h == 0 else cst[h - 1, f, cols - 1, own_rows, :]
            cst[h, f, cols, own_rows, :] = jnp.where(
                lane1 < HALO, a, jnp.where(lane1 >= LANES - HALO, b, 0.0)
            )
    y_copies = [
        to(cst.at[:, :, :, pl.ds(TOP, HALO), :], cst.at[:, :, :, pl.ds(TOP + side, HALO), :],
           y_s.at[0], y_r.at[0], lat=above),
        to(cst.at[:, :, :, pl.ds(TOP + side - HALO, HALO), :],
           cst.at[:, :, :, pl.ds(TOP - HALO, HALO), :],
           y_s.at[1], y_r.at[1], lat=below),
    ]
    for c in y_copies:
        c.start()

    peers(lambda d: planmsg(d, d).wait_recv())
    self_plan.wait()
    plan_copy = pltpu.make_async_copy(plan_all, plan_sm, one_sem.at[2])
    plan_copy.start()
    plan_copy.wait()

    peers(lambda d: stage1(d, d).wait_recv())
    self1.wait()

    def seat(d, j):
        return part[jnp.maximum(plan_sm[d, 0, j], 0)]

    def fill(h, d):
        for j in range(cols):
            block = seat(d, h * cols + j)
            for f in range(3):
                pack[h, d, f * cols + j] = block[f]
        if h == PARTS - 1:
            after = seat(lax.rem(d + 1, n_lon), 0)
        else:
            after = seat(d, (h + 1) * cols)
        if h == 0:
            before = seat(lax.rem(d + n_lon - 1, n_lon), all_cols - 1)
        else:
            before = seat(d, h * cols - 1)
        both = jnp.where(lane1 < LANES // 2, after[0], before[0])
        for f in range(1, 3):
            a = pltpu.roll(after[f], HALO * f, 1)
            b = pltpu.roll(before[f], LANES - HALO * f, 1)
            both = jnp.where((lane1 >= HALO * f) & (lane1 < HALO * (f + 1)), a, both)
            both = jnp.where((lane1 >= LANES - HALO * (f + 1)) & (lane1 < LANES - HALO * f), b, both)
        pack[h, d, 3 * cols] = both

    def stage2(h, d, sender):
        return to(
            pack.at[h, d], sig.at[h, :, rows_of(sender), :],
            p2_s.at[h * n_lon + d], p2_r.at[h * n_lon + sender], lon=d,
        )

    def self2(h):
        return pltpu.make_async_copy(pack.at[h, me], sig.at[h, :, rows_of(me), :], self_sem.at[h])

    for h in range(PARTS):
        def send2(d, h=h):
            fill(h, d)
            stage2(h, d, me).start()
        peers(send2)
        fill(h, me)
        self2(h).start()

    def invert(d, inv):
        for j in range(all_cols):
            inv = jnp.where(lane1 == plan_sm[d, 0, j], d * all_cols + j, inv)
        return inv
    inv_own[...] = lax.fori_loop(0, n_lon, invert, jnp.zeros((1, LANES), jnp.int32))
    inv_copy = pltpu.make_async_copy(inv_own, inv_sm, one_sem.at[3])
    inv_copy.start()

    def east(x):
        r = pltpu.roll(x, LANES - 1, 2)
        return jnp.where(lane == LANES - 1, jnp.concatenate([r[1:], r[:1]], 0), r)

    def west(x):
        r = pltpu.roll(x, 1, 2)
        return jnp.where(lane == 0, jnp.concatenate([r[-1:], r[:-1]], 0), r)

    def diff_x(x):
        return east(x) - west(x)

    def diff_y(ref, h, f, base):
        return ref[h, f, :, pl.ds(base + 1, 8), :] - ref[h, f, :, pl.ds(base - 1, 8), :]

    def increments(h, base, rows):
        u, v = uv[h, 0, :, rows, :], uv[h, 1, :, rows, :]
        ux, vx = diff_x(u), diff_x(v)
        uy, vy = diff_y(uv, h, 0, base), diff_y(uv, h, 1, base)
        div, ten, shr = ux + vy, ux - vy, uy + vx
        a = coef[h, 0, :, rows, :]
        ar = a * lax.rsqrt(div * div + 0.25 * (ten * ten + shr * shr) + 0.25)
        ten4 = 0.25 * ten
        return ar * (div + ten4) - a, ar * (div - ten4) - a, ar * (0.25 * shr)

    def tile(t):
        base = pl.multiple_of(HALO + 8 * t, 8)
        return base, pl.ds(base, 8)

    def loop(lo, hi, fn, unroll=1):
        def step(t, carry):
            fn(*tile(t))
            return carry
        lax.fori_loop(lo, hi, step, 0, unroll=unroll)

    for c in y_copies:
        c.wait_recv()

    def prepare(h, t):
        base, rows = tile(t)
        outside = ((t == 0) & (lat == 0)) | ((t == tiles - 1) & (lat == n_lat - 1))
        mask = cst[h, 6, :, rows, :] * jnp.where(outside, 0.0, 1.0)
        mob = cst[h, 5, :, rows, :]
        ratio = mask / (5.0 + mob)
        push = ratio * mob
        sx, sy = cst[h, 0, :, rows, :], cst[h, 1, :, rows, :]
        uv[h, 0, :, rows, :] = mask * sx
        uv[h, 1, :, rows, :] = mask * sy
        coef[h, 0, :, rows, :] = 0.2 * mask * cst[h, 4, :, rows, :]
        coef[h, 1, :, rows, :] = 4.0 * ratio
        coef[h, 2, :, rows, :] = push
        coef[h, 3, :, rows, :] = ratio * sx + push * cst[h, 2, :, rows, :]
        coef[h, 4, :, rows, :] = ratio * sy + push * cst[h, 3, :, rows, :]
        coef[h, 5, :, rows, :] = mask

    def warm_up(h, carry):
        def step(t, inner):
            prepare(h, t)
            return inner
        lax.fori_loop(0, tiles, step, 0)

        def first(base, rows):
            for f, value in enumerate(increments(h, base, rows)):
                inc[h, f, :, rows, :] = value
        loop(0, tiles, first)
        return carry

    lax.fori_loop(0, PARTS, warm_up, 0)

    def stress_first(h, base, rows):
        w = 0.8 * coef[h, 5, :, rows, :]
        beside = sig[h, 3 * cols, rows, :]
        s = []
        for f in range(3):
            extra = beside
            if f:
                extra = jnp.where(
                    lane1 < LANES // 2,
                    pltpu.roll(beside, LANES - HALO * f, 1), pltpu.roll(beside, HALO * f, 1),
                )
            s.append(jnp.concatenate([sig[h, pl.ds(f * cols, cols), rows, :], extra[None]], 0))
        inc[h, 0, :, rows, :] += w * (s[0] + s[1])
        inc[h, 1, :, rows, :] += w * (s[0] - s[1])
        inc[h, 2, :, rows, :] += (w + w) * s[2]

    def stress_next(h, base, rows):
        for f, value in enumerate(increments(h, base, rows)):
            inc[h, f, :, rows, :] = 0.8 * inc[h, f, :, rows, :] + value

    def momentum(h, base, rows, emit=False):
        fx = 0.25 * (diff_x(inc[h, 0, :, rows, :]) + diff_y(inc, h, 2, base))
        fy = 0.25 * (diff_x(inc[h, 2, :, rows, :]) + diff_y(inc, h, 1, base))
        u, v = uv[h, 0, :, rows, :], uv[h, 1, :, rows, :]
        keep, push = coef[h, 1, :, rows, :], coef[h, 2, :, rows, :]
        un = keep * u + coef[h, 3, :, rows, :] + push * (fx + 0.3 * v)
        vn = keep * v + coef[h, 4, :, rows, :] + push * (fy - 0.3 * u)
        if not emit:
            uv[h, 0, :, rows, :] = un
            uv[h, 1, :, rows, :] = vn
            return
        mask = coef[h, 5, :, rows, :]
        fx, fy = mask * fx, mask * fy
        out_rows = pl.ds(pl.multiple_of(base - TOP, 8), 8)
        for j in range(cols):
            at = pl.ds(pl.multiple_of((h * cols + j) * LANES, LANES), LANES)
            o_vel[0, out_rows, at] = un[j]
            o_vel[1, out_rows, at] = vn[j]
            o_frc[0, out_rows, at] = fx[j]
            o_frc[1, out_rows, at] = fy[j]

    def take(h, sender):
        @pl.when(sender != me)
        def _():
            stage2(h, sender, sender).wait_recv()

        @pl.when(sender == me)
        def _():
            self2(h).wait()

    def piece_tiles(d, fn):
        for i in range(piece // 8):
            base = pl.multiple_of(TOP + d * piece + 8 * i, 8)
            fn(base, pl.ds(base, 8))

    def back1(h, d, sender):
        return to(
            inc.at[h, :, pl.ds(0, cols), rows_of(d), :], back.at[sender, h],
            r1_s.at[h * n_lon + d], r1_r.at[h * n_lon + sender], lon=d,
        )

    def self3(h):
        return pltpu.make_async_copy(
            inc.at[h, :, pl.ds(0, cols), rows_of(me), :], back.at[me, h], self_sem.at[PARTS + h]
        )

    def run(h, carry):
        up = to(sig.at[h, :, pl.ds(TOP, HALO), :], sig.at[h, :, pl.ds(TOP + side, HALO), :],
                h_s.at[2 * h], h_r.at[2 * h], lat=above)
        down = to(sig.at[h, :, pl.ds(TOP + side - HALO, HALO), :],
                  sig.at[h, :, pl.ds(TOP - HALO, HALO), :],
                  h_s.at[2 * h + 1], h_r.at[2 * h + 1], lat=below)
        take(h, 0)
        up.start()
        take(h, n_lon - 1)
        down.start()
        first = functools.partial(stress_first, h)
        move = functools.partial(momentum, h)
        following = functools.partial(stress_next, h)

        def arrive(k, inner):
            sender = lax.rem(me + k * (n_lon - STRIDE % n_lon), n_lon)

            @pl.when((sender != 0) & (sender != n_lon - 1))
            def _():
                take(h, sender)
            piece_tiles(sender, first)
            return inner

        lax.fori_loop(0, n_lon, arrive, 0)
        loop(2, tiles - 2, move, 2)
        up.wait()
        down.wait()
        first(*tile(0))
        first(*tile(tiles - 1))
        for t in (0, 1, tiles - 2, tiles - 1):
            move(*tile(t))

        def subcycle(i, inner):
            loop(0, tiles, following, UNROLL)
            loop(0, tiles, move, UNROLL)
            return inner

        lax.fori_loop(0, NSUB - 2, subcycle, 0)

        def send_back1(d):
            piece_tiles(d, following)
            back1(h, d, me).start()

        peers(send_back1)
        piece_tiles(me, following)
        self3(h).start()
        following(*tile(0))
        following(*tile(tiles - 1))
        return carry

    lax.fori_loop(0, PARTS, run, 0)

    def finish(h, carry):
        loop(1, tiles - 1, functools.partial(momentum, h, emit=True), 2)
        return carry

    lax.fori_loop(0, PARTS, finish, 0)

    inv_copy.wait()
    for h in range(PARTS):
        peers(lambda d, h=h: back1(h, d, d).wait_recv())
        self3(h).wait()

    def refill(d):
        for s in range(slots):
            block = inv_sm[0, d * slots + s]
            owner, column = lax.div(block, all_cols), lax.rem(block, all_cols)
            got = back[owner, lax.div(column, cols), :, lax.rem(column, cols)]
            home[d, s, 0] = 0.5 * (got[0] + got[1])
            home[d, s, 1] = 0.5 * (got[0] - got[1])
            home[d, s, 2] = 0.5 * got[2]

    def back2(d, sender):
        return to(
            home.at[d], o_sig.at[0, :, :, pl.ds(sender * piece, piece), :],
            r2_s.at[d], r2_r.at[sender], lon=d,
        )

    def send_back2(d):
        refill(d)
        back2(d, me).start()

    peers(send_back2)
    refill(me)
    self4 = pltpu.make_async_copy(
        home.at[me], o_sig.at[0, :, :, pl.ds(me * piece, piece), :], one_sem.at[4]
    )
    self4.start()

    for c in x_copies + y_copies:
        c.wait_send()

    def drain(d):
        planmsg(d, me).wait_send()
        stage1(d, me).wait_send()
        for h in range(PARTS):
            stage2(h, d, me).wait_send()
            back1(h, d, me).wait_send()
        back2(d, me).wait_send()

    peers(drain)
    self4.wait()
    peers(lambda d: back2(d, d).wait_recv())


def hand_over(*refs):
    sources, targets, sem = refs[:3], refs[3:6], refs[6]
    moves = [pltpu.make_async_copy(s, t, sem.at[i]) for i, (s, t) in enumerate(zip(sources, targets))]
    for m in moves:
        m.start()
    for m in moves:
        m.wait()


def solution(mesh):
    n_lon, n_lat = mesh.shape["lon"], mesh.shape["lat"]

    def body(velocity_start, forcing, strength, mobility, plan, stress_in):
        cols, slots, side = plan.shape[1], stress_in.shape[1], stress_in.shape[-1]
        cols = cols // PARTS
        piece, wide, tall = side // n_lon, cols + 1, side + 32
        f32, i32 = jnp.float32, jnp.int32
        vmem, dma = pltpu.VMEM, pltpu.SemaphoreType.DMA
        anywhere = pl.BlockSpec(memory_space=pl.ANY)
        inside = pl.BlockSpec(memory_space=pltpu.VMEM)
        shapes = (velocity_start.shape, forcing.shape, stress_in.shape)
        results = pl.pallas_call(
            functools.partial(kernel, n_lon, n_lat),
            out_shape=tuple(vmem(s, f32) for s in shapes),
            in_specs=[pl.BlockSpec(memory_space=pltpu.SMEM)] + [anywhere] * 5,
            out_specs=(inside,) * 3,
            scratch_shapes=[
                vmem((PARTS, 7, wide, tall, LANES), f32),
                vmem((side, LANES), f32),
                vmem((side, LANES), f32),
                vmem((side, LANES), f32),
                vmem((side, LANES), f32),
                vmem((1, LANES), i32),
                vmem((n_lon, 1, LANES), i32),
                pltpu.SMEM((n_lon, 1, LANES), i32),
                vmem((1, LANES), i32),
                pltpu.SMEM((1, LANES), i32),
                vmem((n_lon * slots, 3, piece, LANES), f32),
                vmem((PARTS, n_lon, 3 * cols + 1, piece, LANES), f32),
                vmem((PARTS, 3 * cols + 1, tall, LANES), f32),
                vmem((PARTS, 2, wide, tall, LANES), f32),
                vmem((PARTS, 6, wide, tall, LANES), f32),
                vmem((PARTS, 3, wide, tall, LANES), f32),
                vmem((n_lon, PARTS, 3, cols, piece, LANES), f32),
                vmem((n_lon, slots, 3, piece, LANES), f32),
                dma((4 * cols * PARTS,)),
                dma((5,)),
                dma((2 * PARTS,)),
                dma((n_lon,)), dma((n_lon,)),
                dma((n_lon,)), dma((n_lon,)),
                dma((2,)), dma((2,)),
                dma((2,)), dma((2,)),
                dma((PARTS * n_lon,)), dma((PARTS * n_lon,)),
                dma((2 * PARTS,)), dma((2 * PARTS,)),
                dma((PARTS * n_lon,)), dma((PARTS * n_lon,)),
                dma((n_lon,)), dma((n_lon,)),
            ],
            compiler_params=pltpu.CompilerParams(collective_id=0, has_side_effects=True),
        )(plan, velocity_start, forcing, strength, mobility, stress_in)
        return tuple(pl.pallas_call(
            hand_over,
            out_shape=tuple(jax.ShapeDtypeStruct(s, f32) for s in shapes),
            in_specs=[inside] * 3,
            out_specs=(pl.BlockSpec(memory_space=pltpu.HBM),) * 3,
            scratch_shapes=[dma((3,))],
            compiler_params=pltpu.CompilerParams(vmem_limit_bytes=1 << 20),
        )(*results))

    placed = (
        P(None, "lat", "lon"),
        P(None, "lat", "lon"),
        P("lat", "lon"),
        P("lat", "lon"),
        P("lat", "lon"),
        P("lat", "lon", None, None, None),
    )
    return jax.shard_map(
        body,
        mesh=mesh,
        in_specs=placed,
        out_specs=(P(None, "lat", "lon"), P(None, "lat", "lon"), P("lat", "lon", None, None, None)),
        check_vma=False,
    )
```

```python
import functools

import jax
import jax.numpy as jnp
from jax import lax
from jax.experimental import pallas as pl
from jax.experimental.pallas import tpu as pltpu
from jax.sharding import PartitionSpec as P

NSUB = 4
PARTS = 2
STRIDE = 3
DEPTH = 5
DECAY = 0.8
LANES = 128
HALO = 8
TOP = 16
MESH = pl.DeviceIdType.MESH


def kernel(
    n_lon, n_lat,
    plan_ref, vel_ref, frc_ref, str_ref, mob_ref, sig_ref,
    o_vel, o_frc, o_sig,
    cst, edge_l, edge_r, halo_r, halo_l,
    plan_own, plan_all, plan_sm, inv_own, inv_sm,
    part, pack, sig, uv, coef, inc, back, home,
    loc_sem, one_sem, self_sem, p1_s, p1_r, pl_s, pl_r, x_s, x_r, y_s, y_r,
    p2_s, p2_r, h_s, h_r, r1_s, r1_r, r2_s, r2_r,
):
    me = lax.axis_index("lon")
    lat = lax.axis_index("lat")
    right, left = lax.rem(me + 1, n_lon), lax.rem(me + n_lon - 1, n_lon)
    below, above = lax.rem(lat + 1, n_lat), lax.rem(lat + n_lat - 1, n_lat)
    side = LANES
    all_cols = plan_ref.shape[1]
    cols = all_cols // PARTS
    slots = sig_ref.shape[1]
    piece = side // n_lon
    tiles = (side + 2 * HALO) // 8
    lane1 = lax.broadcasted_iota(jnp.int32, (1, LANES), 1)
    lane = lax.broadcasted_iota(jnp.int32, (1, 1, LANES), 2)

    def to(src, dst, ss, rs, **where):
        return pltpu.make_async_remote_copy(
            src_ref=src, dst_ref=dst, send_sem=ss, recv_sem=rs,
            device_id=where, device_id_type=MESH,
        )

    def peers(fn):
        def step(k, carry):
            fn(lax.rem(me + k * STRIDE, n_lon))
            return carry
        lax.fori_loop(1, n_lon, step, 0)

    def rows_of(d):
        return pl.ds(TOP + d * piece, piece)

    barrier = pltpu.get_barrier_semaphore()
    peers(lambda d: pl.semaphore_signal(barrier, inc=1, device_id={"lon": d}, device_id_type=MESH))
    for other in (above, below):
        pl.semaphore_signal(barrier, inc=1, device_id={"lat": other}, device_id_type=MESH)

    own_rows = pl.ds(TOP, side)
    copies = []
    for j in range(all_cols):
        h, t = divmod(j, cols)
        src_cols = pl.ds(j * LANES, LANES)
        copies += [
            (vel_ref.at[:, :, src_cols], cst.at[h, pl.ds(0, 2), t, own_rows, :]),
            (frc_ref.at[:, :, src_cols], cst.at[h, pl.ds(2, 2), t, own_rows, :]),
            (str_ref.at[:, src_cols], cst.at[h, 4, t, own_rows, :]),
            (mob_ref.at[:, src_cols], cst.at[h, 5, t, own_rows, :]),
        ]
    copies = [pltpu.make_async_copy(s, d, loc_sem.at[i]) for i, (s, d) in enumerate(copies)]
    for c in copies:
        c.start()
    row = jnp.full((1, LANES), -1, jnp.int32)
    for j in range(all_cols):
        h, t = divmod(j, cols)
        row = jnp.where(lane1 == j, plan_ref[0, j], row)
        active = jnp.where(plan_ref[0, j] >= 0, 1.0, 0.0)
        cst[h, 6, t, own_rows, :] = jnp.full((side, LANES), active, jnp.float32)
    plan_own[...] = row
    for c in copies:
        c.wait()

    to_left = jnp.zeros((side, LANES), jnp.float32)
    to_right = jnp.zeros((side, LANES), jnp.float32)
    for f in range(7):
        first, last = cst[0, f, 0, own_rows, :], cst[PARTS - 1, f, cols - 1, own_rows, :]
        if f:
            first = pltpu.roll(first, HALO * f, 1)
            last = pltpu.roll(last, LANES - HALO * f, 1)
        to_left = jnp.where((lane1 >= HALO * f) & (lane1 < HALO * (f + 1)), first, to_left)
        to_right = jnp.where(
            (lane1 >= LANES - HALO * (f + 1)) & (lane1 < LANES - HALO * f), last, to_right
        )
    edge_l[...] = to_left
    edge_r[...] = to_right
    pl.semaphore_wait(barrier, n_lon + 1)

    def stage1(d, sender):
        return to(
            sig_ref.at[0, :, :, pl.ds(d * piece, piece), :],
            part.at[pl.ds(sender * slots, slots)],
            p1_s.at[d], p1_r.at[sender], lon=d,
        )

    def planmsg(d, sender):
        return to(plan_own, plan_all.at[sender], pl_s.at[d], pl_r.at[sender], lon=d)

    x_copies = [
        to(edge_l, halo_r, x_s.at[0], x_r.at[0], lon=left),
        to(edge_r, halo_l, x_s.at[1], x_r.at[1], lon=right),
    ]
    for c in x_copies:
        c.start()
    peers(lambda d: planmsg(d, me).start())
    peers(lambda d: stage1(d, me).start())
    self1 = pltpu.make_async_copy(
        sig_ref.at[0, :, :, pl.ds(me * piece, piece), :],
        part.at[pl.ds(me * slots, slots)], one_sem.at[0],
    )
    self1.start()
    self_plan = pltpu.make_async_copy(plan_own, plan_all.at[me], one_sem.at[1])
    self_plan.start()

    for c in x_copies:
        c.wait_recv()
    for f in range(7):
        from_r, from_l = halo_r[...], halo_l[...]
        if f:
            from_r = pltpu.roll(from_r, LANES - HALO * f, 1)
            from_l = pltpu.roll(from_l, HALO * f, 1)
        for h in range(PARTS):
            a = from_r if h == PARTS - 1 else cst[h + 1, f, 0, own_rows, :]
            b = from_l if h == 0 else cst[h - 1, f, cols - 1, own_rows, :]
            cst[h, f, cols, own_rows, :] = jnp.where(
                lane1 < HALO, a, jnp.where(lane1 >= LANES - HALO, b, 0.0)
            )
    y_copies = [
        to(cst.at[:, :, :, pl.ds(TOP, HALO), :], cst.at[:, :, :, pl.ds(TOP + side, HALO), :],
           y_s.at[0], y_r.at[0], lat=above),
        to(cst.at[:, :, :, pl.ds(TOP + side - HALO, HALO), :],
           cst.at[:, :, :, pl.ds(TOP - HALO, HALO), :],
           y_s.at[1], y_r.at[1], lat=below),
    ]
    for c in y_copies:
        c.start()

    peers(lambda d: planmsg(d, d).wait_recv())
    self_plan.wait()
    plan_copy = pltpu.make_async_copy(plan_all, plan_sm, one_sem.at[2])
    plan_copy.start()
    plan_copy.wait()

    peers(lambda d: stage1(d, d).wait_recv())
    self1.wait()

    def seat(d, j):
        return part[jnp.maximum(plan_sm[d, 0, j], 0)]

    def fill(h, d):
        for j in range(cols):
            block = seat(d, h * cols + j)
            for f in range(3):
                pack[h, d, f * cols + j] = block[f]
        if h == PARTS - 1:
            after = seat(lax.rem(d + 1, n_lon), 0)
        else:
            after = seat(d, (h + 1) * cols)
        if h == 0:
            before = seat(lax.rem(d + n_lon - 1, n_lon), all_cols - 1)
        else:
            before = seat(d, h * cols - 1)
        both = jnp.where(lane1 < LANES // 2, after[0], before[0])
        for f in range(1, 3):
            a = pltpu.roll(after[f], HALO * f, 1)
            b = pltpu.roll(before[f], LANES - HALO * f, 1)
            both = jnp.where((lane1 >= HALO * f) & (lane1 < HALO * (f + 1)), a, both)
            both = jnp.where((lane1 >= LANES - HALO * (f + 1)) & (lane1 < LANES - HALO * f), b, both)
        pack[h, d, 3 * cols] = both

    def stage2(h, d, sender):
        return to(
            pack.at[h, d], sig.at[h, :, rows_of(sender), :],
            p2_s.at[h * n_lon + d], p2_r.at[h * n_lon + sender], lon=d,
        )

    def self2(h):
        return pltpu.make_async_copy(pack.at[h, me], sig.at[h, :, rows_of(me), :], self_sem.at[h])

    for h in range(PARTS):
        def send2(d, h=h):
            fill(h, d)
            stage2(h, d, me).start()
        peers(send2)
        fill(h, me)
        self2(h).start()

    def invert(d, inv):
        for j in range(all_cols):
            inv = jnp.where(lane1 == plan_sm[d, 0, j], d * all_cols + j, inv)
        return inv
    inv_own[...] = lax.fori_loop(0, n_lon, invert, jnp.zeros((1, LANES), jnp.int32))
    inv_copy = pltpu.make_async_copy(inv_own, inv_sm, one_sem.at[3])
    inv_copy.start()

    def east(x):
        r = pltpu.roll(x, LANES - 1, 2)
        return jnp.where(lane == LANES - 1, jnp.concatenate([r[1:], r[:1]], 0), r)

    def west(x):
        r = pltpu.roll(x, 1, 2)
        return jnp.where(lane == 0, jnp.concatenate([r[-1:], r[:-1]], 0), r)

    def diff_x(x):
        return east(x) - west(x)

    def diff_y(ref, h, f, base):
        return ref[h, f, :, pl.ds(base + 1, 8), :] - ref[h, f, :, pl.ds(base - 1, 8), :]

    def increments(h, k, base, rows):
        u, v = uv[h, 0, :, rows, :], uv[h, 1, :, rows, :]
        ux, vx = diff_x(u), diff_x(v)
        uy, vy = diff_y(uv, h, 0, base), diff_y(uv, h, 1, base)
        div, ten, shr = ux + vy, ux - vy, uy + vx
        a = DECAY ** -k * coef[h, 0, :, rows, :]
        ar = a * lax.rsqrt(div * div + 0.25 * (ten * ten + shr * shr) + 0.25)
        ten4 = 0.25 * ten
        return ar * (div + ten4) - a, ar * (div - ten4) - a, ar * (0.25 * shr)

    def tile(t):
        base = pl.multiple_of(HALO + 8 * t, 8)
        return base, pl.ds(base, 8)

    def loop(lo, hi, fn, unroll=1):
        def step(t, carry):
            fn(*tile(t))
            return carry
        lax.fori_loop(lo, hi, step, 0, unroll=unroll)

    for c in y_copies:
        c.wait_recv()

    def prepare(h, t):
        base, rows = tile(t)
        outside = ((t == 0) & (lat == 0)) | ((t == tiles - 1) & (lat == n_lat - 1))
        mask = cst[h, 6, :, rows, :] * jnp.where(outside, 0.0, 1.0)
        mob = cst[h, 5, :, rows, :]
        ratio = mask / (5.0 + mob)
        push = ratio * mob
        sx, sy = cst[h, 0, :, rows, :], cst[h, 1, :, rows, :]
        uv[h, 0, :, rows, :] = mask * sx
        uv[h, 1, :, rows, :] = mask * sy
        coef[h, 0, :, rows, :] = 0.2 * mask * cst[h, 4, :, rows, :]
        coef[h, 1, :, rows, :] = 4.0 * ratio
        coef[h, 2, :, rows, :] = push
        coef[h, 3, :, rows, :] = ratio * sx + push * cst[h, 2, :, rows, :]
        coef[h, 4, :, rows, :] = ratio * sy + push * cst[h, 3, :, rows, :]
        coef[h, 5, :, rows, :] = mask

    def warm_up(h, carry):
        def step(t, inner):
            prepare(h, t)
            return inner
        lax.fori_loop(0, tiles, step, 0)

        def first(base, rows):
            for f, value in enumerate(increments(h, 1, base, rows)):
                inc[h, f, :, rows, :] = value
        loop(0, tiles, first, 6)
        return carry

    lax.fori_loop(0, PARTS, warm_up, 0)

    def stress_first(h, base, rows):
        w = coef[h, 5, :, rows, :]
        beside = sig[h, 3 * cols, rows, :]
        s = []
        for f in range(3):
            extra = beside
            if f:
                extra = jnp.where(
                    lane1 < LANES // 2,
                    pltpu.roll(beside, LANES - HALO * f, 1), pltpu.roll(beside, HALO * f, 1),
                )
            s.append(jnp.concatenate([sig[h, pl.ds(f * cols, cols), rows, :], extra[None]], 0))
        inc[h, 0, :, rows, :] += w * (s[0] + s[1])
        inc[h, 1, :, rows, :] += w * (s[0] - s[1])
        inc[h, 2, :, rows, :] += (w + w) * s[2]

    def stress_next(h, k, base, rows):
        for f, value in enumerate(increments(h, k, base, rows)):
            inc[h, f, :, rows, :] += value

    def momentum(h, k, base, rows, emit=False):
        scale = 0.25 * DECAY ** k
        fx = diff_x(inc[h, 0, :, rows, :]) + diff_y(inc, h, 2, base)
        fy = diff_x(inc[h, 2, :, rows, :]) + diff_y(inc, h, 1, base)
        u, v = uv[h, 0, :, rows, :], uv[h, 1, :, rows, :]
        keep, push = coef[h, 1, :, rows, :], scale * coef[h, 2, :, rows, :]
        turn = 0.3 / scale
        un = keep * u + coef[h, 3, :, rows, :] + push * (fx + turn * v)
        vn = keep * v + coef[h, 4, :, rows, :] + push * (fy - turn * u)
        if not emit:
            uv[h, 0, :, rows, :] = un
            uv[h, 1, :, rows, :] = vn
            return
        mask = scale * coef[h, 5, :, rows, :]
        fx, fy = mask * fx, mask * fy
        out_rows = pl.ds(pl.multiple_of(base - TOP, 8), 8)
        for j in range(cols):
            at = pl.ds(pl.multiple_of((h * cols + j) * LANES, LANES), LANES)
            o_vel[0, out_rows, at] = un[j]
            o_vel[1, out_rows, at] = vn[j]
            o_frc[0, out_rows, at] = fx[j]
            o_frc[1, out_rows, at] = fy[j]

    def take(h, sender):
        @pl.when(sender != me)
        def _():
            stage2(h, sender, sender).wait_recv()

        @pl.when(sender == me)
        def _():
            self2(h).wait()

    def piece_tiles(d, fn):
        for i in range(piece // 8):
            base = pl.multiple_of(TOP + d * piece + 8 * i, 8)
            fn(base, pl.ds(base, 8))

    def back1(h, d, sender):
        return to(
            inc.at[h, :, pl.ds(0, cols), rows_of(d), :], back.at[sender, h],
            r1_s.at[h * n_lon + d], r1_r.at[h * n_lon + sender], lon=d,
        )

    def self3(h):
        return pltpu.make_async_copy(
            inc.at[h, :, pl.ds(0, cols), rows_of(me), :], back.at[me, h], self_sem.at[PARTS + h]
        )

    def run(h, carry):
        up = to(sig.at[h, :, pl.ds(TOP, HALO), :], sig.at[h, :, pl.ds(TOP + side, HALO), :],
                h_s.at[2 * h], h_r.at[2 * h], lat=above)
        down = to(sig.at[h, :, pl.ds(TOP + side - HALO, HALO), :],
                  sig.at[h, :, pl.ds(TOP - HALO, HALO), :],
                  h_s.at[2 * h + 1], h_r.at[2 * h + 1], lat=below)
        take(h, 0)
        up.start()
        take(h, n_lon - 1)
        down.start()
        first = functools.partial(stress_first, h)
        stages = []
        for k in range(1, NSUB):
            stages += [functools.partial(momentum, h, k), functools.partial(stress_next, h, k + 1)]

        def arrive(k, inner):
            sender = lax.rem(me + k * (n_lon - STRIDE % n_lon), n_lon)

            @pl.when((sender != 0) & (sender != n_lon - 1))
            def _():
                take(h, sender)
            piece_tiles(sender, first)
            return inner

        lax.fori_loop(0, n_lon, arrive, 0)
        for i in range(DEPTH):
            loop(2 + i, tiles - 2 - i, stages[i], tiles - 4 - 2 * i)
        up.wait()
        down.wait()
        first(*tile(0))
        first(*tile(tiles - 1))
        for i, stage in enumerate(stages):
            if i < DEPTH:
                loop(0, 2 + i, stage, 2 + i)
                loop(tiles - 2 - i, tiles, stage, 2 + i)
            else:
                loop(0, tiles, stage, tiles)
        peers(lambda d: back1(h, d, me).start())
        self3(h).start()
        return carry

    lax.fori_loop(0, PARTS, run, 0)

    def finish(h, carry):
        loop(1, tiles - 1, functools.partial(momentum, h, NSUB, emit=True), 8)
        return carry

    lax.fori_loop(0, PARTS, finish, 0)

    inv_copy.wait()
    for h in range(PARTS):
        peers(lambda d, h=h: back1(h, d, d).wait_recv())
        self3(h).wait()

    def refill(d):
        for s in range(slots):
            block = inv_sm[0, d * slots + s]
            owner, column = lax.div(block, all_cols), lax.rem(block, all_cols)
            got = back[owner, lax.div(column, cols), :, lax.rem(column, cols)]
            got = (0.5 * DECAY ** NSUB) * got
            home[d, s, 0] = got[0] + got[1]
            home[d, s, 1] = got[0] - got[1]
            home[d, s, 2] = got[2]

    def back2(d, sender):
        return to(
            home.at[d], o_sig.at[0, :, :, pl.ds(sender * piece, piece), :],
            r2_s.at[d], r2_r.at[sender], lon=d,
        )

    def send_back2(d):
        refill(d)
        back2(d, me).start()

    peers(send_back2)
    refill(me)
    self4 = pltpu.make_async_copy(
        home.at[me], o_sig.at[0, :, :, pl.ds(me * piece, piece), :], one_sem.at[4]
    )
    self4.start()

    for c in x_copies + y_copies:
        c.wait_send()

    def drain(d):
        planmsg(d, me).wait_send()
        stage1(d, me).wait_send()
        for h in range(PARTS):
            stage2(h, d, me).wait_send()
            back1(h, d, me).wait_send()
        back2(d, me).wait_send()

    peers(drain)
    self4.wait()
    peers(lambda d: back2(d, d).wait_recv())


def hand_over(*refs):
    sources, targets, sem = refs[:3], refs[3:6], refs[6]
    moves = [pltpu.make_async_copy(s, t, sem.at[i]) for i, (s, t) in enumerate(zip(sources, targets))]
    for m in moves:
        m.start()
    for m in moves:
        m.wait()


def solution(mesh):
    n_lon, n_lat = mesh.shape["lon"], mesh.shape["lat"]

    def body(velocity_start, forcing, strength, mobility, plan, stress_in):
        cols, slots, side = plan.shape[1], stress_in.shape[1], stress_in.shape[-1]
        cols = cols // PARTS
        piece, wide, tall = side // n_lon, cols + 1, side + 32
        f32, i32 = jnp.float32, jnp.int32
        vmem, dma = pltpu.VMEM, pltpu.SemaphoreType.DMA
        anywhere = pl.BlockSpec(memory_space=pl.ANY)
        inside = pl.BlockSpec(memory_space=pltpu.VMEM)
        shapes = (velocity_start.shape, forcing.shape, stress_in.shape)
        results = pl.pallas_call(
            functools.partial(kernel, n_lon, n_lat),
            out_shape=tuple(vmem(s, f32) for s in shapes),
            in_specs=[pl.BlockSpec(memory_space=pltpu.SMEM)] + [anywhere] * 5,
            out_specs=(inside,) * 3,
            scratch_shapes=[
                vmem((PARTS, 7, wide, tall, LANES), f32),
                vmem((side, LANES), f32),
                vmem((side, LANES), f32),
                vmem((side, LANES), f32),
                vmem((side, LANES), f32),
                vmem((1, LANES), i32),
                vmem((n_lon, 1, LANES), i32),
                pltpu.SMEM((n_lon, 1, LANES), i32),
                vmem((1, LANES), i32),
                pltpu.SMEM((1, LANES), i32),
                vmem((n_lon * slots, 3, piece, LANES), f32),
                vmem((PARTS, n_lon, 3 * cols + 1, piece, LANES), f32),
                vmem((PARTS, 3 * cols + 1, tall, LANES), f32),
                vmem((PARTS, 2, wide, tall, LANES), f32),
                vmem((PARTS, 6, wide, tall, LANES), f32),
                vmem((PARTS, 3, wide, tall, LANES), f32),
                vmem((n_lon, PARTS, 3, cols, piece, LANES), f32),
                vmem((n_lon, slots, 3, piece, LANES), f32),
                dma((4 * cols * PARTS,)),
                dma((5,)),
                dma((2 * PARTS,)),
                dma((n_lon,)), dma((n_lon,)),
                dma((n_lon,)), dma((n_lon,)),
                dma((2,)), dma((2,)),
                dma((2,)), dma((2,)),
                dma((PARTS * n_lon,)), dma((PARTS * n_lon,)),
                dma((2 * PARTS,)), dma((2 * PARTS,)),
                dma((PARTS * n_lon,)), dma((PARTS * n_lon,)),
                dma((n_lon,)), dma((n_lon,)),
            ],
            compiler_params=pltpu.CompilerParams(collective_id=0, has_side_effects=True),
        )(plan, velocity_start, forcing, strength, mobility, stress_in)
        return tuple(pl.pallas_call(
            hand_over,
            out_shape=tuple(jax.ShapeDtypeStruct(s, f32) for s in shapes),
            in_specs=[inside] * 3,
            out_specs=(pl.BlockSpec(memory_space=pltpu.HBM),) * 3,
            scratch_shapes=[dma((3,))],
            compiler_params=pltpu.CompilerParams(vmem_limit_bytes=1 << 20),
        )(*results))

    placed = (
        P(None, "lat", "lon"),
        P(None, "lat", "lon"),
        P("lat", "lon"),
        P("lat", "lon"),
        P("lat", "lon"),
        P("lat", "lon", None, None, None),
    )
    return jax.shard_map(
        body,
        mesh=mesh,
        in_specs=placed,
        out_specs=(P(None, "lat", "lon"), P(None, "lat", "lon"), P("lat", "lon", None, None, None)),
        check_vma=False,
    )
```

```python
import functools

import jax
import jax.numpy as jnp
from jax import lax
from jax.experimental import pallas as pl
from jax.experimental.pallas import tpu as pltpu
from jax.sharding import PartitionSpec as P

NSUB = 4
PARTS = 2
FAR_FIRST = (10, 6, 14, 9, 11, 2, 8, 5, 15, 7, 13, 1, 4, 3, 12)
DEPTH = 5
DECAY = 0.8
LANES = 128
HALO = 8
TOP = 16
MESH = pl.DeviceIdType.MESH
SPLIT = (pl.ds(2, 1), pl.ds(0, 2))


def kernel(
    n_lon, n_lat,
    plan_ref, vel_ref, frc_ref, str_ref, mob_ref, sig_ref,
    o_vel, o_frc, o_sig,
    cst, edge_l, edge_r, halo_r, halo_l,
    plan_own, plan_all, plan_sm, inv_own, inv_sm,
    part_a, part_b, pack, sig, uv, coef, inc, back_a, back_b, home,
    loc_sem, one_sem, first_sem, self_sem, p1_s, p1_r, pl_s, pl_r, x_s, x_r, y_s, y_r,
    p2_s, p2_r, h_s, h_r, r1_s, r1_r, r2_s, r2_r,
):
    me = lax.axis_index("lon")
    lat = lax.axis_index("lat")
    right, left = lax.rem(me + 1, n_lon), lax.rem(me + n_lon - 1, n_lon)
    below, above = lax.rem(lat + 1, n_lat), lax.rem(lat + n_lat - 1, n_lat)
    side = LANES
    all_cols = plan_ref.shape[1]
    cols = all_cols // PARTS
    slots = sig_ref.shape[1]
    piece = side // n_lon
    tiles = (side + 2 * HALO) // 8
    lane1 = lax.broadcasted_iota(jnp.int32, (1, LANES), 1)
    lane = lax.broadcasted_iota(jnp.int32, (1, 1, LANES), 2)

    def to(src, dst, ss, rs, **where):
        return pltpu.make_async_remote_copy(
            src_ref=src, dst_ref=dst, send_sem=ss, recv_sem=rs,
            device_id=where, device_id_type=MESH,
        )

    def each(fn):
        def step(k, carry):
            fn(lax.rem(me + k, n_lon))
            return carry
        lax.fori_loop(1, n_lon, step, 0)

    if n_lon == 16:
        y, x = lax.div(me, 4), lax.rem(me, 4)
        ahead = [4 * lax.rem(y + i // 4, 4) + lax.rem(x + i % 4, 4) for i in FAR_FIRST]
        behind = [4 * lax.rem(y + 4 - i // 4, 4) + lax.rem(x + 4 - i % 4, 4) for i in FAR_FIRST]
    else:
        ahead = [lax.rem(me + i, n_lon) for i in range(1, n_lon)]
        behind = [lax.rem(me + n_lon - i, n_lon) for i in range(1, n_lon)]

    def peers(fn, sign=1):
        for d in ahead if sign > 0 else behind:
            fn(d)

    def rows_of(d):
        return pl.ds(TOP + d * piece, piece)

    barrier = pltpu.get_barrier_semaphore()
    each(lambda d: pl.semaphore_signal(barrier, inc=1, device_id={"lon": d}, device_id_type=MESH))
    for other in (above, below):
        pl.semaphore_signal(barrier, inc=1, device_id={"lat": other}, device_id_type=MESH)

    own_rows = pl.ds(TOP, side)
    copies = []
    for j in range(all_cols):
        h, t = divmod(j, cols)
        src_cols = pl.ds(j * LANES, LANES)
        copies += [
            (vel_ref.at[:, :, src_cols], cst.at[h, pl.ds(0, 2), t, own_rows, :]),
            (frc_ref.at[:, :, src_cols], cst.at[h, pl.ds(2, 2), t, own_rows, :]),
            (str_ref.at[:, src_cols], cst.at[h, 4, t, own_rows, :]),
            (mob_ref.at[:, src_cols], cst.at[h, 5, t, own_rows, :]),
        ]
    copies = [pltpu.make_async_copy(s, d, loc_sem.at[i]) for i, (s, d) in enumerate(copies)]
    for c in copies:
        c.start()
    row = jnp.full((1, LANES), -1, jnp.int32)
    for j in range(all_cols):
        h, t = divmod(j, cols)
        row = jnp.where(lane1 == j, plan_ref[0, j], row)
        active = jnp.where(plan_ref[0, j] >= 0, 1.0, 0.0)
        cst[h, 6, t, own_rows, :] = jnp.full((side, LANES), active, jnp.float32)
    plan_own[...] = row
    for c in copies:
        c.wait()

    to_left = jnp.zeros((side, LANES), jnp.float32)
    to_right = jnp.zeros((side, LANES), jnp.float32)
    for f in range(7):
        first, last = cst[0, f, 0, own_rows, :], cst[PARTS - 1, f, cols - 1, own_rows, :]
        if f:
            first = pltpu.roll(first, HALO * f, 1)
            last = pltpu.roll(last, LANES - HALO * f, 1)
        to_left = jnp.where((lane1 >= HALO * f) & (lane1 < HALO * (f + 1)), first, to_left)
        to_right = jnp.where(
            (lane1 >= LANES - HALO * (f + 1)) & (lane1 < LANES - HALO * f), last, to_right
        )
    half = side // 2
    low = lane1 < LANES // 2
    edge_l[...] = jnp.where(low, to_left[:half], pltpu.roll(to_left[half:], LANES // 2, 1))
    edge_r[...] = jnp.where(low, pltpu.roll(to_right[half:], LANES // 2, 1), to_right[:half])
    pl.semaphore_wait(barrier, n_lon + 1)

    part, back = (part_a, part_b), (back_a, back_b)

    def stage1(c, d, sender):
        fields = SPLIT[c]
        return to(
            sig_ref.at[0, :, fields, pl.ds(d * piece, piece), :],
            part[c].at[pl.ds(sender * slots, slots)],
            p1_s.at[c * n_lon + d], p1_r.at[c * n_lon + sender], lon=d,
        )

    def planmsg(d, sender):
        return to(plan_own, plan_all.at[sender], pl_s.at[d], pl_r.at[sender], lon=d)

    x_copies = [
        to(edge_l, halo_r, x_s.at[0], x_r.at[0], lon=left),
        to(edge_r, halo_l, x_s.at[1], x_r.at[1], lon=right),
    ]
    for c in x_copies:
        c.start()
    each(lambda d: planmsg(d, me).start())
    for c in range(2):
        peers(lambda d, c=c: stage1(c, d, me).start())
    self1 = [
        pltpu.make_async_copy(
            sig_ref.at[0, :, SPLIT[c], pl.ds(me * piece, piece), :],
            part[c].at[pl.ds(me * slots, slots)], first_sem.at[c],
        )
        for c in range(2)
    ]
    for c in self1:
        c.start()
    self_plan = pltpu.make_async_copy(plan_own, plan_all.at[me], one_sem.at[1])
    self_plan.start()

    for c in x_copies:
        c.wait_recv()
    for f in range(7):
        from_r, from_l = (
            jnp.concatenate([got[...], pltpu.roll(got[...], LANES // 2, 1)], 0) for got in (halo_r, halo_l)
        )
        if f:
            from_r = pltpu.roll(from_r, LANES - HALO * f, 1)
            from_l = pltpu.roll(from_l, HALO * f, 1)
        for h in range(PARTS):
            a = from_r if h == PARTS - 1 else cst[h + 1, f, 0, own_rows, :]
            b = from_l if h == 0 else cst[h - 1, f, cols - 1, own_rows, :]
            cst[h, f, cols, own_rows, :] = jnp.where(
                lane1 < HALO, a, jnp.where(lane1 >= LANES - HALO, b, 0.0)
            )
    y_copies = [
        to(cst.at[:, :, :, pl.ds(TOP, HALO), :], cst.at[:, :, :, pl.ds(TOP + side, HALO), :],
           y_s.at[0], y_r.at[0], lat=above),
        to(cst.at[:, :, :, pl.ds(TOP + side - HALO, HALO), :],
           cst.at[:, :, :, pl.ds(TOP - HALO, HALO), :],
           y_s.at[1], y_r.at[1], lat=below),
    ]
    for c in y_copies:
        c.start()

    each(lambda d: planmsg(d, d).wait_recv())
    self_plan.wait()
    plan_copy = pltpu.make_async_copy(plan_all, plan_sm, one_sem.at[2])
    plan_copy.start()
    plan_copy.wait()

    for c in self1:
        c.wait()

    def seat(c, d, j):
        return part[c][jnp.maximum(plan_sm[d, 0, j], 0)]

    def fill_first(h, d):
        for j in range(cols):
            pack[h, d, j] = seat(0, d, h * cols + j)[0]

    def fill_rest(h, d):
        for j in range(cols):
            block = seat(1, d, h * cols + j)
            pack[h, d, cols + j] = block[0]
            pack[h, d, 2 * cols + j] = block[1]
        if h:
            return
        both = jnp.zeros((piece, LANES), jnp.float32)
        for g in range(PARTS):
            after = (d, (g + 1) * cols) if g < PARTS - 1 else (lax.rem(d + 1, n_lon), 0)
            before = (d, g * cols - 1) if g else (lax.rem(d + n_lon - 1, n_lon), all_cols - 1)
            for f in range(3):
                i = 3 * g + f
                c, at = (1, f) if f < 2 else (0, 0)
                a, b = seat(c, *after)[at], seat(c, *before)[at]
                if i:
                    a, b = pltpu.roll(a, HALO * i, 1), pltpu.roll(b, LANES - HALO * i, 1)
                both = jnp.where((lane1 >= HALO * i) & (lane1 < HALO * (i + 1)), a, both)
                both = jnp.where((lane1 >= LANES - HALO * (i + 1)) & (lane1 < LANES - HALO * i), b, both)
        pack[0, d, 3 * cols] = both

    def width(h):
        return 3 * cols + (1 if h == 0 else 0)

    def stage2(h, c, d, sender):
        span = pl.ds(0, cols) if c == 0 else pl.ds(cols, width(h) - cols)
        slot = (2 * h + c) * n_lon
        return to(
            pack.at[h, d, span], sig.at[h, span, rows_of(sender), :],
            p2_s.at[slot + d], p2_r.at[slot + sender], lon=d,
        )

    def self2(h):
        span = pl.ds(0, width(h))
        return pltpu.make_async_copy(
            pack.at[h, me, span], sig.at[h, span, rows_of(me), :], self_sem.at[h]
        )

    for c, fill in enumerate((fill_first, fill_rest)):
        each(lambda d, c=c: stage1(c, d, d).wait_recv())
        for h in range(PARTS):
            def send2(d, h=h, c=c, fill=fill):
                fill(h, d)
                stage2(h, c, d, me).start()
            peers(send2)
            fill(h, me)
            if c == 1:
                self2(h).start()

    def invert(d, inv):
        for j in range(all_cols):
            inv = jnp.where(lane1 == plan_sm[d, 0, j], d * all_cols + j, inv)
        return inv
    inv_own[...] = lax.fori_loop(0, n_lon, invert, jnp.zeros((1, LANES), jnp.int32))
    inv_copy = pltpu.make_async_copy(inv_own, inv_sm, one_sem.at[3])
    inv_copy.start()

    def east(x):
        r = pltpu.roll(x, LANES - 1, 2)
        return jnp.where(lane == LANES - 1, jnp.concatenate([r[1:], r[:1]], 0), r)

    def west(x):
        r = pltpu.roll(x, 1, 2)
        return jnp.where(lane == 0, jnp.concatenate([r[-1:], r[:-1]], 0), r)

    def diff_x(x):
        return east(x) - west(x)

    def diff_y(ref, h, f, base):
        return ref[h, f, :, pl.ds(base + 1, 8), :] - ref[h, f, :, pl.ds(base - 1, 8), :]

    def increments(h, k, base, rows):
        u, v = uv[h, 0, :, rows, :], uv[h, 1, :, rows, :]
        ux, vx = diff_x(u), diff_x(v)
        uy, vy = diff_y(uv, h, 0, base), diff_y(uv, h, 1, base)
        div, ten, shr = ux + vy, ux - vy, uy + vx
        a = DECAY ** -k * coef[h, 0, :, rows, :]
        ar = a * lax.rsqrt(div * div + 0.25 * (ten * ten + shr * shr) + 0.25)
        ten4 = 0.25 * ten
        return ar * (div + ten4) - a, ar * (div - ten4) - a, ar * (0.25 * shr)

    def tile(t):
        base = pl.multiple_of(HALO + 8 * t, 8)
        return base, pl.ds(base, 8)

    def loop(lo, hi, fn, unroll=1):
        def step(t, carry):
            fn(*tile(t))
            return carry
        lax.fori_loop(lo, hi, step, 0, unroll=unroll)

    for c in y_copies:
        c.wait_recv()

    def prepare(h, t):
        base, rows = tile(t)
        outside = ((t == 0) & (lat == 0)) | ((t == tiles - 1) & (lat == n_lat - 1))
        mask = cst[h, 6, :, rows, :] * jnp.where(outside, 0.0, 1.0)
        mob = cst[h, 5, :, rows, :]
        ratio = mask / (5.0 + mob)
        push = ratio * mob
        sx, sy = cst[h, 0, :, rows, :], cst[h, 1, :, rows, :]
        uv[h, 0, :, rows, :] = mask * sx
        uv[h, 1, :, rows, :] = mask * sy
        coef[h, 0, :, rows, :] = 0.2 * mask * cst[h, 4, :, rows, :]
        coef[h, 1, :, rows, :] = 4.0 * ratio
        coef[h, 2, :, rows, :] = push
        coef[h, 3, :, rows, :] = ratio * sx + push * cst[h, 2, :, rows, :]
        coef[h, 4, :, rows, :] = ratio * sy + push * cst[h, 3, :, rows, :]
        coef[h, 5, :, rows, :] = mask

    def warm_up(h, carry):
        def step(t, inner):
            prepare(h, t)
            return inner
        lax.fori_loop(0, tiles, step, 0)

        def first(base, rows):
            for f, value in enumerate(increments(h, 1, base, rows)):
                inc[h, f, :, rows, :] = value
        loop(0, tiles, first, 6)
        return carry

    lax.fori_loop(0, PARTS, warm_up, 0)

    def stress_first(h, base, rows):
        w = coef[h, 5, :, rows, :]
        beside = sig[0, 3 * cols, rows, :]
        s = []
        for f in range(3):
            i, at = 3 * h + f, (1, 2, 0)[f] * cols
            extra = beside
            if i:
                extra = jnp.where(
                    lane1 < LANES // 2,
                    pltpu.roll(beside, LANES - HALO * i, 1), pltpu.roll(beside, HALO * i, 1),
                )
            s.append(jnp.concatenate([sig[h, pl.ds(at, cols), rows, :], extra[None]], 0))
        inc[h, 0, :, rows, :] += w * (s[0] + s[1])
        inc[h, 1, :, rows, :] += w * (s[0] - s[1])
        inc[h, 2, :, rows, :] += (w + w) * s[2]

    def stress_next(h, k, base, rows):
        for f, value in enumerate(increments(h, k, base, rows)):
            inc[h, f, :, rows, :] += value

    def momentum(h, k, base, rows, emit=False):
        scale = 0.25 * DECAY ** k
        fx = diff_x(inc[h, 0, :, rows, :]) + diff_y(inc, h, 2, base)
        fy = diff_x(inc[h, 2, :, rows, :]) + diff_y(inc, h, 1, base)
        u, v = uv[h, 0, :, rows, :], uv[h, 1, :, rows, :]
        keep, push = coef[h, 1, :, rows, :], scale * coef[h, 2, :, rows, :]
        turn = 0.3 / scale
        un = keep * u + coef[h, 3, :, rows, :] + push * (fx + turn * v)
        vn = keep * v + coef[h, 4, :, rows, :] + push * (fy - turn * u)
        if not emit:
            uv[h, 0, :, rows, :] = un
            uv[h, 1, :, rows, :] = vn
            return
        mask = scale * coef[h, 5, :, rows, :]
        fx, fy = mask * fx, mask * fy
        out_rows = pl.ds(pl.multiple_of(base - TOP, 8), 8)
        for j in range(cols):
            at = pl.ds(pl.multiple_of((h * cols + j) * LANES, LANES), LANES)
            o_vel[0, out_rows, at] = un[j]
            o_vel[1, out_rows, at] = vn[j]
            o_frc[0, out_rows, at] = fx[j]
            o_frc[1, out_rows, at] = fy[j]

    def take(h, sender):
        @pl.when(sender != me)
        def _():
            for c in range(2):
                stage2(h, c, sender, sender).wait_recv()

        @pl.when(sender == me)
        def _():
            self2(h).wait()

    def piece_tiles(d, fn):
        for i in range(piece // 8):
            base = pl.multiple_of(TOP + d * piece + 8 * i, 8)
            fn(base, pl.ds(base, 8))

    def back1(h, c, d, sender):
        fields, slot = SPLIT[c], (2 * h + c) * n_lon
        return to(
            inc.at[h, fields, pl.ds(0, cols), rows_of(d), :], back[c].at[sender, h],
            r1_s.at[slot + d], r1_r.at[slot + sender], lon=d,
        )

    def self3(h, c):
        return pltpu.make_async_copy(
            inc.at[h, SPLIT[c], pl.ds(0, cols), rows_of(me), :], back[c].at[me, h],
            self_sem.at[PARTS + 2 * h + c],
        )

    def run(h):
        span = pl.ds(0, width(h))
        up = to(sig.at[h, span, pl.ds(TOP, HALO), :], sig.at[h, span, pl.ds(TOP + side, HALO), :],
                h_s.at[2 * h], h_r.at[2 * h], lat=above)
        down = to(sig.at[h, span, pl.ds(TOP + side - HALO, HALO), :],
                  sig.at[h, span, pl.ds(TOP - HALO, HALO), :],
                  h_s.at[2 * h + 1], h_r.at[2 * h + 1], lat=below)
        take(h, 0)
        up.start()
        take(h, n_lon - 1)
        down.start()
        first = functools.partial(stress_first, h)
        stages = []
        for k in range(1, NSUB):
            stages += [functools.partial(momentum, h, k), functools.partial(stress_next, h, k + 1)]

        def arrive(sender):
            @pl.when((sender != 0) & (sender != n_lon - 1))
            def _():
                take(h, sender)
            piece_tiles(sender, first)

        peers(arrive, -1)
        arrive(me)
        for i in range(DEPTH):
            loop(2 + i, tiles - 2 - i, stages[i], tiles - 4 - 2 * i)
        up.wait()
        down.wait()
        first(*tile(0))
        first(*tile(tiles - 1))
        for i, stage in enumerate(stages):
            if i < DEPTH:
                loop(0, 2 + i, stage, 2 + i)
                loop(tiles - 2 - i, tiles, stage, 2 + i)
            else:
                loop(0, tiles, stage, tiles)
        for c in range(2):
            peers(lambda d, c=c: back1(h, c, d, me).start())
        for c in range(2):
            self3(h, c).start()

    for h in range(PARTS):
        run(h)

    def finish(h, carry):
        loop(1, tiles - 1, functools.partial(momentum, h, NSUB, emit=True), 8)
        return carry

    lax.fori_loop(0, PARTS, finish, 0)

    def refill(c, d):
        for s in range(slots):
            block = inv_sm[0, d * slots + s]
            owner, column = lax.div(block, all_cols), lax.rem(block, all_cols)
            h, j = lax.div(column, cols), lax.rem(column, cols)
            scale = 0.5 * DECAY ** NSUB
            if c == 0:
                home[d, s, 2] = scale * back[0][owner, h, 0, j]
            if c == 1:
                plus, minus = scale * back[1][owner, h, 0, j], scale * back[1][owner, h, 1, j]
                home[d, s, 0] = plus + minus
                home[d, s, 1] = plus - minus

    def back2(c, d, sender):
        fields = SPLIT[c]
        return to(
            home.at[d, :, fields], o_sig.at[0, :, fields, pl.ds(sender * piece, piece), :],
            r2_s.at[c * n_lon + d], r2_r.at[c * n_lon + sender], lon=d,
        )

    inv_copy.wait()
    for h in range(PARTS):
        for c in range(2):
            self3(h, c).wait()
    for c in range(2):
        for h in range(PARTS):
            each(lambda d, h=h, c=c: back1(h, c, d, d).wait_recv())

        def send_back2(d, c=c):
            refill(c, d)
            back2(c, d, me).start()

        peers(send_back2)
        refill(c, me)
    self4 = pltpu.make_async_copy(
        home.at[me], o_sig.at[0, :, :, pl.ds(me * piece, piece), :], one_sem.at[4]
    )
    self4.start()

    for c in x_copies + y_copies:
        c.wait_send()

    def drain(d):
        planmsg(d, me).wait_send()
        for c in range(2):
            stage1(c, d, me).wait_send()
            for h in range(PARTS):
                stage2(h, c, d, me).wait_send()
        for c in range(2):
            for h in range(PARTS):
                back1(h, c, d, me).wait_send()
            back2(c, d, me).wait_send()

    each(drain)
    self4.wait()
    for c in range(2):
        each(lambda d, c=c: back2(c, d, d).wait_recv())


def hand_over(*refs):
    sources, targets, sem = refs[:3], refs[3:6], refs[6]
    moves = [pltpu.make_async_copy(s, t, sem.at[i]) for i, (s, t) in enumerate(zip(sources, targets))]
    for m in moves:
        m.start()
    for m in moves:
        m.wait()


def solution(mesh):
    n_lon, n_lat = mesh.shape["lon"], mesh.shape["lat"]

    def body(velocity_start, forcing, strength, mobility, plan, stress_in):
        cols, slots, side = plan.shape[1], stress_in.shape[1], stress_in.shape[-1]
        cols = cols // PARTS
        piece, wide, tall = side // n_lon, cols + 1, side + 32
        f32, i32 = jnp.float32, jnp.int32
        vmem, dma = pltpu.VMEM, pltpu.SemaphoreType.DMA
        anywhere = pl.BlockSpec(memory_space=pl.ANY)
        inside = pl.BlockSpec(memory_space=pltpu.VMEM)
        shapes = (velocity_start.shape, forcing.shape, stress_in.shape)
        results = pl.pallas_call(
            functools.partial(kernel, n_lon, n_lat),
            out_shape=tuple(vmem(s, f32) for s in shapes),
            in_specs=[pl.BlockSpec(memory_space=pltpu.SMEM)] + [anywhere] * 5,
            out_specs=(inside,) * 3,
            scratch_shapes=[
                vmem((PARTS, 7, wide, tall, LANES), f32),
                vmem((side // 2, LANES), f32),
                vmem((side // 2, LANES), f32),
                vmem((side // 2, LANES), f32),
                vmem((side // 2, LANES), f32),
                vmem((1, LANES), i32),
                vmem((n_lon, 1, LANES), i32),
                pltpu.SMEM((n_lon, 1, LANES), i32),
                vmem((1, LANES), i32),
                pltpu.SMEM((1, LANES), i32),
                vmem((n_lon * slots, 1, piece, LANES), f32),
                vmem((n_lon * slots, 2, piece, LANES), f32),
                vmem((PARTS, n_lon, 3 * cols + 1, piece, LANES), f32),
                vmem((PARTS, 3 * cols + 1, tall, LANES), f32),
                vmem((PARTS, 2, wide, tall, LANES), f32),
                vmem((PARTS, 6, wide, tall, LANES), f32),
                vmem((PARTS, 3, wide, tall, LANES), f32),
                vmem((n_lon, PARTS, 1, cols, piece, LANES), f32),
                vmem((n_lon, PARTS, 2, cols, piece, LANES), f32),
                vmem((n_lon, slots, 3, piece, LANES), f32),
                dma((4 * cols * PARTS,)),
                dma((5,)),
                dma((2,)),
                dma((3 * PARTS,)),
                dma((2 * n_lon,)), dma((2 * n_lon,)),
                dma((n_lon,)), dma((n_lon,)),
                dma((2,)), dma((2,)),
                dma((2,)), dma((2,)),
                dma((2 * PARTS * n_lon,)), dma((2 * PARTS * n_lon,)),
                dma((2 * PARTS,)), dma((2 * PARTS,)),
                dma((2 * PARTS * n_lon,)), dma((2 * PARTS * n_lon,)),
                dma((2 * n_lon,)), dma((2 * n_lon,)),
            ],
            compiler_params=pltpu.CompilerParams(collective_id=0, has_side_effects=True),
        )(plan, velocity_start, forcing, strength, mobility, stress_in)
        return tuple(pl.pallas_call(
            hand_over,
            out_shape=tuple(jax.ShapeDtypeStruct(s, f32) for s in shapes),
            in_specs=[inside] * 3,
            out_specs=(pl.BlockSpec(memory_space=pltpu.HBM),) * 3,
            scratch_shapes=[dma((3,))],
            compiler_params=pltpu.CompilerParams(vmem_limit_bytes=1 << 20),
        )(*results))

    placed = (
        P(None, "lat", "lon"),
        P(None, "lat", "lon"),
        P("lat", "lon"),
        P("lat", "lon"),
        P("lat", "lon"),
        P("lat", "lon", None, None, None),
    )
    return jax.shard_map(
        body,
        mesh=mesh,
        in_specs=placed,
        out_specs=(P(None, "lat", "lon"), P(None, "lat", "lon"), P("lat", "lon", None, None, None)),
        check_vma=False,
    )
```

```python
import functools

import jax
import jax.numpy as jnp
from jax import lax
from jax.experimental import pallas as pl
from jax.experimental.pallas import tpu as pltpu
from jax.sharding import PartitionSpec as P

NSUB = 4
PARTS = 2
FAR_FIRST = (10, 9, 11, 6, 14, 5, 15, 7, 13, 2, 8, 1, 3, 4, 12)
DEPTH = 5
DECAY = 0.8
LANES = 128
HALO = 8
TOP = 16
MESH = pl.DeviceIdType.MESH
SPLIT = (pl.ds(2, 1), pl.ds(0, 2))


def kernel(
    n_lon, n_lat,
    plan_ref, vel_ref, frc_ref, str_ref, mob_ref, sig_ref,
    o_vel, o_frc, o_sig,
    cst, edge_l, edge_r, halo_r, halo_l,
    plan_own, plan_all, plan_sm, inv_own, inv_sm,
    part_a, part_b, pack, sig, uv, coef, inc, back_a, back_b, home,
    loc_sem, one_sem, first_sem, self_sem, p1_s, p1_r, pl_s, pl_r, x_s, x_r, y_s, y_r,
    p2_s, p2_r, h_s, h_r, r1_s, r1_r, r2_s, r2_r,
):
    me = lax.axis_index("lon")
    lat = lax.axis_index("lat")
    right, left = lax.rem(me + 1, n_lon), lax.rem(me + n_lon - 1, n_lon)
    below, above = lax.rem(lat + 1, n_lat), lax.rem(lat + n_lat - 1, n_lat)
    side = LANES
    all_cols = plan_ref.shape[1]
    cols = all_cols // PARTS
    slots = sig_ref.shape[1]
    piece = side // n_lon
    tiles = (side + 2 * HALO) // 8
    lane1 = lax.broadcasted_iota(jnp.int32, (1, LANES), 1)
    lane = lax.broadcasted_iota(jnp.int32, (1, 1, LANES), 2)

    def to(src, dst, ss, rs, **where):
        return pltpu.make_async_remote_copy(
            src_ref=src, dst_ref=dst, send_sem=ss, recv_sem=rs,
            device_id=where, device_id_type=MESH,
        )

    def each(fn):
        def step(k, carry):
            fn(lax.rem(me + k, n_lon))
            return carry
        lax.fori_loop(1, n_lon, step, 0)

    if n_lon == 16:
        y, x = lax.div(me, 4), lax.rem(me, 4)
        ahead = [4 * lax.rem(y + i // 4, 4) + lax.rem(x + i % 4, 4) for i in FAR_FIRST]
        behind = [4 * lax.rem(y + 4 - i // 4, 4) + lax.rem(x + 4 - i % 4, 4) for i in FAR_FIRST]
    else:
        ahead = [lax.rem(me + i, n_lon) for i in range(1, n_lon)]
        behind = [lax.rem(me + n_lon - i, n_lon) for i in range(1, n_lon)]

    def peers(fn, sign=1):
        for d in ahead if sign > 0 else behind:
            fn(d)

    def rows_of(d):
        return pl.ds(TOP + d * piece, piece)

    barrier = pltpu.get_barrier_semaphore()
    peers(lambda d: pl.semaphore_signal(barrier, inc=1, device_id={"lon": d}, device_id_type=MESH))
    for other in (above, below):
        pl.semaphore_signal(barrier, inc=1, device_id={"lat": other}, device_id_type=MESH)

    own_rows = pl.ds(TOP, side)
    copies = []
    for j in range(all_cols):
        h, t = divmod(j, cols)
        src_cols = pl.ds(j * LANES, LANES)
        copies += [
            (vel_ref.at[:, :, src_cols], cst.at[h, pl.ds(0, 2), t, own_rows, :]),
            (frc_ref.at[:, :, src_cols], cst.at[h, pl.ds(2, 2), t, own_rows, :]),
            (str_ref.at[:, src_cols], cst.at[h, 4, t, own_rows, :]),
            (mob_ref.at[:, src_cols], cst.at[h, 5, t, own_rows, :]),
        ]
    copies = [pltpu.make_async_copy(s, d, loc_sem.at[i]) for i, (s, d) in enumerate(copies)]
    for c in copies:
        c.start()
    row = jnp.full((1, LANES), -1, jnp.int32)
    for j in range(all_cols):
        h, t = divmod(j, cols)
        row = jnp.where(lane1 == j, plan_ref[0, j], row)
        active = jnp.where(plan_ref[0, j] >= 0, 1.0, 0.0)
        cst[h, 6, t, own_rows, :] = jnp.full((side, LANES), active, jnp.float32)
    plan_own[...] = row
    for c in copies:
        c.wait()

    to_left = jnp.zeros((side, LANES), jnp.float32)
    to_right = jnp.zeros((side, LANES), jnp.float32)
    for f in range(7):
        first, last = cst[0, f, 0, own_rows, :], cst[PARTS - 1, f, cols - 1, own_rows, :]
        if f:
            first = pltpu.roll(first, HALO * f, 1)
            last = pltpu.roll(last, LANES - HALO * f, 1)
        to_left = jnp.where((lane1 >= HALO * f) & (lane1 < HALO * (f + 1)), first, to_left)
        to_right = jnp.where(
            (lane1 >= LANES - HALO * (f + 1)) & (lane1 < LANES - HALO * f), last, to_right
        )
    half = side // 2
    low = lane1 < LANES // 2
    edge_l[...] = jnp.where(low, to_left[:half], pltpu.roll(to_left[half:], LANES // 2, 1))
    edge_r[...] = jnp.where(low, pltpu.roll(to_right[half:], LANES // 2, 1), to_right[:half])
    pl.semaphore_wait(barrier, n_lon + 1)

    part, back = (part_a, part_b), (back_a, back_b)

    def stage1(c, d, sender):
        fields = SPLIT[c]
        return to(
            sig_ref.at[0, :, fields, pl.ds(d * piece, piece), :],
            part[c].at[pl.ds(sender * slots, slots)],
            p1_s.at[c * n_lon + d], p1_r.at[c * n_lon + sender], lon=d,
        )

    def planmsg(d, sender):
        return to(plan_own, plan_all.at[sender], pl_s.at[d], pl_r.at[sender], lon=d)

    x_copies = [
        to(edge_l, halo_r, x_s.at[0], x_r.at[0], lon=left),
        to(edge_r, halo_l, x_s.at[1], x_r.at[1], lon=right),
    ]
    for c in x_copies:
        c.start()
    each(lambda d: planmsg(d, me).start())
    for c in range(2):
        peers(lambda d, c=c: stage1(c, d, me).start())
    self1 = [
        pltpu.make_async_copy(
            sig_ref.at[0, :, SPLIT[c], pl.ds(me * piece, piece), :],
            part[c].at[pl.ds(me * slots, slots)], first_sem.at[c],
        )
        for c in range(2)
    ]
    for c in self1:
        c.start()
    self_plan = pltpu.make_async_copy(plan_own, plan_all.at[me], one_sem.at[1])
    self_plan.start()

    for c in x_copies:
        c.wait_recv()
    for f in range(7):
        from_r, from_l = (
            jnp.concatenate([got[...], pltpu.roll(got[...], LANES // 2, 1)], 0) for got in (halo_r, halo_l)
        )
        if f:
            from_r = pltpu.roll(from_r, LANES - HALO * f, 1)
            from_l = pltpu.roll(from_l, HALO * f, 1)
        for h in range(PARTS):
            a = from_r if h == PARTS - 1 else cst[h + 1, f, 0, own_rows, :]
            b = from_l if h == 0 else cst[h - 1, f, cols - 1, own_rows, :]
            cst[h, f, cols, own_rows, :] = jnp.where(
                lane1 < HALO, a, jnp.where(lane1 >= LANES - HALO, b, 0.0)
            )
    y_copies = [
        to(cst.at[:, :, :, pl.ds(TOP, HALO), :], cst.at[:, :, :, pl.ds(TOP + side, HALO), :],
           y_s.at[0], y_r.at[0], lat=above),
        to(cst.at[:, :, :, pl.ds(TOP + side - HALO, HALO), :],
           cst.at[:, :, :, pl.ds(TOP - HALO, HALO), :],
           y_s.at[1], y_r.at[1], lat=below),
    ]
    for c in y_copies:
        c.start()

    each(lambda d: planmsg(d, d).wait_recv())
    self_plan.wait()
    plan_copy = pltpu.make_async_copy(plan_all, plan_sm, one_sem.at[2])
    plan_copy.start()
    plan_copy.wait()

    for c in self1:
        c.wait()

    def seat(c, d, j):
        return part[c][jnp.maximum(plan_sm[d, 0, j], 0)]

    def fill_first(h, d):
        for j in range(cols):
            pack[h, d, j] = seat(0, d, h * cols + j)[0]

    def fill_rest(h, d):
        for j in range(cols):
            block = seat(1, d, h * cols + j)
            pack[h, d, cols + j] = block[0]
            pack[h, d, 2 * cols + j] = block[1]
        if h:
            return
        both = jnp.zeros((piece, LANES), jnp.float32)
        for g in range(PARTS):
            after = (d, (g + 1) * cols) if g < PARTS - 1 else (lax.rem(d + 1, n_lon), 0)
            before = (d, g * cols - 1) if g else (lax.rem(d + n_lon - 1, n_lon), all_cols - 1)
            for f in range(3):
                i = 3 * g + f
                c, at = (1, f) if f < 2 else (0, 0)
                a, b = seat(c, *after)[at], seat(c, *before)[at]
                if i:
                    a, b = pltpu.roll(a, HALO * i, 1), pltpu.roll(b, LANES - HALO * i, 1)
                both = jnp.where((lane1 >= HALO * i) & (lane1 < HALO * (i + 1)), a, both)
                both = jnp.where((lane1 >= LANES - HALO * (i + 1)) & (lane1 < LANES - HALO * i), b, both)
        pack[0, d, 3 * cols] = both

    def width(h):
        return 3 * cols + (1 if h == 0 else 0)

    def stage2(h, c, d, sender):
        span = pl.ds(0, cols) if c == 0 else pl.ds(cols, width(h) - cols)
        slot = (2 * h + c) * n_lon
        if c == 0:
            return to(
                pack.at[:, d, span], sig.at[:, span, rows_of(sender), :],
                p2_s.at[d], p2_r.at[sender], lon=d,
            )
        return to(
            pack.at[h, d, span], sig.at[h, span, rows_of(sender), :],
            p2_s.at[slot + d], p2_r.at[slot + sender], lon=d,
        )

    def self2(h):
        span = pl.ds(0, width(h))
        return pltpu.make_async_copy(
            pack.at[h, me, span], sig.at[h, span, rows_of(me), :], self_sem.at[h]
        )

    def send_first(d):
        for h in range(PARTS):
            fill_first(h, d)
        stage2(0, 0, d, me).start()

    each(lambda d: stage1(0, d, d).wait_recv())
    peers(send_first)
    for h in range(PARTS):
        fill_first(h, me)
    each(lambda d: stage1(1, d, d).wait_recv())
    for h in range(PARTS):
        def send_rest(d, h=h):
            fill_rest(h, d)
            stage2(h, 1, d, me).start()
        peers(send_rest)
        fill_rest(h, me)
        self2(h).start()

    def invert(d, inv):
        for j in range(all_cols):
            inv = jnp.where(lane1 == plan_sm[d, 0, j], d * all_cols + j, inv)
        return inv
    inv_own[...] = lax.fori_loop(0, n_lon, invert, jnp.zeros((1, LANES), jnp.int32))
    inv_copy = pltpu.make_async_copy(inv_own, inv_sm, one_sem.at[3])
    inv_copy.start()

    def east(x):
        r = pltpu.roll(x, LANES - 1, 2)
        return jnp.where(lane == LANES - 1, jnp.concatenate([r[1:], r[:1]], 0), r)

    def west(x):
        r = pltpu.roll(x, 1, 2)
        return jnp.where(lane == 0, jnp.concatenate([r[-1:], r[:-1]], 0), r)

    def diff_x(x):
        return east(x) - west(x)

    def diff_y(ref, h, f, base):
        return ref[h, f, :, pl.ds(base + 1, 8), :] - ref[h, f, :, pl.ds(base - 1, 8), :]

    def increments(h, k, base, rows):
        u, v = uv[h, 0, :, rows, :], uv[h, 1, :, rows, :]
        ux, vx = diff_x(u), diff_x(v)
        uy, vy = diff_y(uv, h, 0, base), diff_y(uv, h, 1, base)
        div, ten, shr = ux + vy, ux - vy, uy + vx
        a = DECAY ** -k * coef[h, 0, :, rows, :]
        ar = a * lax.rsqrt(div * div + 0.25 * (ten * ten + shr * shr) + 0.25)
        ten4 = 0.25 * ten
        return ar * (div + ten4) - a, ar * (div - ten4) - a, ar * (0.25 * shr)

    def tile(t):
        base = pl.multiple_of(HALO + 8 * t, 8)
        return base, pl.ds(base, 8)

    def loop(lo, hi, fn, unroll=1):
        def step(t, carry):
            fn(*tile(t))
            return carry
        lax.fori_loop(lo, hi, step, 0, unroll=unroll)

    for c in y_copies:
        c.wait_recv()

    def prepare(h, t):
        base, rows = tile(t)
        outside = ((t == 0) & (lat == 0)) | ((t == tiles - 1) & (lat == n_lat - 1))
        mask = cst[h, 6, :, rows, :] * jnp.where(outside, 0.0, 1.0)
        mob = cst[h, 5, :, rows, :]
        ratio = mask / (5.0 + mob)
        push = ratio * mob
        sx, sy = cst[h, 0, :, rows, :], cst[h, 1, :, rows, :]
        uv[h, 0, :, rows, :] = mask * sx
        uv[h, 1, :, rows, :] = mask * sy
        coef[h, 0, :, rows, :] = 0.2 * mask * cst[h, 4, :, rows, :]
        coef[h, 1, :, rows, :] = 4.0 * ratio
        coef[h, 2, :, rows, :] = push
        coef[h, 3, :, rows, :] = ratio * sx + push * cst[h, 2, :, rows, :]
        coef[h, 4, :, rows, :] = ratio * sy + push * cst[h, 3, :, rows, :]
        coef[h, 5, :, rows, :] = mask

    def warm_up(h, carry):
        def step(t, inner):
            prepare(h, t)
            return inner
        lax.fori_loop(0, tiles, step, 0, unroll=6)

        def first(base, rows):
            for f, value in enumerate(increments(h, 1, base, rows)):
                inc[h, f, :, rows, :] = value
        loop(0, tiles, first, 6)
        return carry

    lax.fori_loop(0, PARTS, warm_up, 0)

    def stress_first(h, base, rows):
        w = coef[h, 5, :, rows, :]
        beside = sig[0, 3 * cols, rows, :]
        s = []
        for f in range(3):
            i, at = 3 * h + f, (1, 2, 0)[f] * cols
            extra = beside
            if i:
                extra = jnp.where(
                    lane1 < LANES // 2,
                    pltpu.roll(beside, LANES - HALO * i, 1), pltpu.roll(beside, HALO * i, 1),
                )
            s.append(jnp.concatenate([sig[h, pl.ds(at, cols), rows, :], extra[None]], 0))
        inc[h, 0, :, rows, :] += w * (s[0] + s[1])
        inc[h, 1, :, rows, :] += w * (s[0] - s[1])
        inc[h, 2, :, rows, :] += (w + w) * s[2]

    def stress_next(h, k, base, rows):
        for f, value in enumerate(increments(h, k, base, rows)):
            inc[h, f, :, rows, :] += value

    def momentum(h, k, base, rows, emit=False):
        scale = 0.25 * DECAY ** k
        fx = diff_x(inc[h, 0, :, rows, :]) + diff_y(inc, h, 2, base)
        fy = diff_x(inc[h, 2, :, rows, :]) + diff_y(inc, h, 1, base)
        u, v = uv[h, 0, :, rows, :], uv[h, 1, :, rows, :]
        keep, push = coef[h, 1, :, rows, :], scale * coef[h, 2, :, rows, :]
        turn = 0.3 / scale
        un = keep * u + coef[h, 3, :, rows, :] + push * (fx + turn * v)
        vn = keep * v + coef[h, 4, :, rows, :] + push * (fy - turn * u)
        if not emit:
            uv[h, 0, :, rows, :] = un
            uv[h, 1, :, rows, :] = vn
            return
        mask = scale * coef[h, 5, :, rows, :]
        fx, fy = mask * fx, mask * fy
        out_rows = pl.ds(pl.multiple_of(base - TOP, 8), 8)
        for j in range(cols):
            at = pl.ds(pl.multiple_of((h * cols + j) * LANES, LANES), LANES)
            o_vel[0, out_rows, at] = un[j]
            o_vel[1, out_rows, at] = vn[j]
            o_frc[0, out_rows, at] = fx[j]
            o_frc[1, out_rows, at] = fy[j]

    def take(h, sender):
        @pl.when(sender != me)
        def _():
            if h == 0:
                stage2(0, 0, sender, sender).wait_recv()
            stage2(h, 1, sender, sender).wait_recv()

        @pl.when(sender == me)
        def _():
            self2(h).wait()

    def piece_tiles(d, fn):
        for i in range(piece // 8):
            base = pl.multiple_of(TOP + d * piece + 8 * i, 8)
            fn(base, pl.ds(base, 8))

    def back1(h, c, d, sender):
        fields, slot = SPLIT[c], (2 * h + c) * n_lon
        return to(
            inc.at[h, fields, pl.ds(0, cols), rows_of(d), :], back[c].at[sender, h],
            r1_s.at[slot + d], r1_r.at[slot + sender], lon=d,
        )

    def self3(h, c):
        return pltpu.make_async_copy(
            inc.at[h, SPLIT[c], pl.ds(0, cols), rows_of(me), :], back[c].at[me, h],
            self_sem.at[PARTS + 2 * h + c],
        )

    def run(h):
        span = pl.ds(0, width(h))
        up = to(sig.at[h, span, pl.ds(TOP, HALO), :], sig.at[h, span, pl.ds(TOP + side, HALO), :],
                h_s.at[2 * h], h_r.at[2 * h], lat=above)
        down = to(sig.at[h, span, pl.ds(TOP + side - HALO, HALO), :],
                  sig.at[h, span, pl.ds(TOP - HALO, HALO), :],
                  h_s.at[2 * h + 1], h_r.at[2 * h + 1], lat=below)
        take(h, 0)
        up.start()
        take(h, n_lon - 1)
        down.start()
        first = functools.partial(stress_first, h)
        stages = []
        for k in range(1, NSUB):
            stages += [functools.partial(momentum, h, k), functools.partial(stress_next, h, k + 1)]

        def arrive(sender):
            @pl.when((sender != 0) & (sender != n_lon - 1))
            def _():
                take(h, sender)
            piece_tiles(sender, first)

        peers(arrive, -1)
        arrive(me)
        for i in range(DEPTH):
            loop(2 + i, tiles - 2 - i, stages[i], tiles - 4 - 2 * i)
        up.wait()
        down.wait()
        first(*tile(0))
        first(*tile(tiles - 1))
        for i, stage in enumerate(stages):
            if i < DEPTH:
                loop(0, 2 + i, stage, 2 + i)
                loop(tiles - 2 - i, tiles, stage, 2 + i)
            else:
                loop(0, tiles, stage, tiles)
        for c in range(2):
            peers(lambda d, c=c: back1(h, c, d, me).start())
        for c in range(2):
            self3(h, c).start()

    for h in range(PARTS):
        run(h)

    def finish(h, carry):
        loop(1, tiles - 1, functools.partial(momentum, h, NSUB, emit=True), 8)
        return carry

    lax.fori_loop(0, PARTS, finish, 0)

    def refill(c, d):
        for s in range(slots):
            block = inv_sm[0, d * slots + s]
            owner, column = lax.div(block, all_cols), lax.rem(block, all_cols)
            h, j = lax.div(column, cols), lax.rem(column, cols)
            scale = 0.5 * DECAY ** NSUB
            if c == 0:
                home[d, s, 2] = scale * back[0][owner, h, 0, j]
            if c == 1:
                plus, minus = scale * back[1][owner, h, 0, j], scale * back[1][owner, h, 1, j]
                home[d, s, 0] = plus + minus
                home[d, s, 1] = plus - minus

    def back2(c, d, sender):
        fields = SPLIT[c]
        return to(
            home.at[d, :, fields], o_sig.at[0, :, fields, pl.ds(sender * piece, piece), :],
            r2_s.at[c * n_lon + d], r2_r.at[c * n_lon + sender], lon=d,
        )

    inv_copy.wait()
    for h in range(PARTS):
        for c in range(2):
            self3(h, c).wait()
    for c in range(2):
        for h in range(PARTS):
            each(lambda d, h=h, c=c: back1(h, c, d, d).wait_recv())

        def send_back2(d, c=c):
            refill(c, d)
            back2(c, d, me).start()

        peers(send_back2)
        refill(c, me)
    self4 = pltpu.make_async_copy(
        home.at[me], o_sig.at[0, :, :, pl.ds(me * piece, piece), :], one_sem.at[4]
    )
    self4.start()

    for c in x_copies + y_copies:
        c.wait_send()

    def drain(d):
        planmsg(d, me).wait_send()
        stage2(0, 0, d, me).wait_send()
        for h in range(PARTS):
            stage2(h, 1, d, me).wait_send()
        for c in range(2):
            stage1(c, d, me).wait_send()
        for c in range(2):
            for h in range(PARTS):
                back1(h, c, d, me).wait_send()
            back2(c, d, me).wait_send()

    each(drain)
    self4.wait()
    for c in range(2):
        each(lambda d, c=c: back2(c, d, d).wait_recv())


def hand_over(*refs):
    sources, targets, sem = refs[:3], refs[3:6], refs[6]
    moves = [pltpu.make_async_copy(s, t, sem.at[i]) for i, (s, t) in enumerate(zip(sources, targets))]
    for m in moves:
        m.start()
    for m in moves:
        m.wait()


def solution(mesh):
    n_lon, n_lat = mesh.shape["lon"], mesh.shape["lat"]

    def body(velocity_start, forcing, strength, mobility, plan, stress_in):
        cols, slots, side = plan.shape[1], stress_in.shape[1], stress_in.shape[-1]
        cols = cols // PARTS
        piece, wide, tall = side // n_lon, cols + 1, side + 32
        f32, i32 = jnp.float32, jnp.int32
        vmem, dma = pltpu.VMEM, pltpu.SemaphoreType.DMA
        anywhere = pl.BlockSpec(memory_space=pl.ANY)
        inside = pl.BlockSpec(memory_space=pltpu.VMEM)
        shapes = (velocity_start.shape, forcing.shape, stress_in.shape)
        results = pl.pallas_call(
            functools.partial(kernel, n_lon, n_lat),
            out_shape=tuple(vmem(s, f32) for s in shapes),
            in_specs=[pl.BlockSpec(memory_space=pltpu.SMEM)] + [anywhere] * 5,
            out_specs=(inside,) * 3,
            scratch_shapes=[
                vmem((PARTS, 7, wide, tall, LANES), f32),
                vmem((side // 2, LANES), f32),
                vmem((side // 2, LANES), f32),
                vmem((side // 2, LANES), f32),
                vmem((side // 2, LANES), f32),
                vmem((1, LANES), i32),
                vmem((n_lon, 1, LANES), i32),
                pltpu.SMEM((n_lon, 1, LANES), i32),
                vmem((1, LANES), i32),
                pltpu.SMEM((1, LANES), i32),
                vmem((n_lon * slots, 1, piece, LANES), f32),
                vmem((n_lon * slots, 2, piece, LANES), f32),
                vmem((PARTS, n_lon, 3 * cols + 1, piece, LANES), f32),
                vmem((PARTS, 3 * cols + 1, tall, LANES), f32),
                vmem((PARTS, 2, wide, tall, LANES), f32),
                vmem((PARTS, 6, wide, tall, LANES), f32),
                vmem((PARTS, 3, wide, tall, LANES), f32),
                vmem((n_lon, PARTS, 1, cols, piece, LANES), f32),
                vmem((n_lon, PARTS, 2, cols, piece, LANES), f32),
                vmem((n_lon, slots, 3, piece, LANES), f32),
                dma((4 * cols * PARTS,)),
                dma((5,)),
                dma((2,)),
                dma((3 * PARTS,)),
                dma((2 * n_lon,)), dma((2 * n_lon,)),
                dma((n_lon,)), dma((n_lon,)),
                dma((2,)), dma((2,)),
                dma((2,)), dma((2,)),
                dma((2 * PARTS * n_lon,)), dma((2 * PARTS * n_lon,)),
                dma((2 * PARTS,)), dma((2 * PARTS,)),
                dma((2 * PARTS * n_lon,)), dma((2 * PARTS * n_lon,)),
                dma((2 * n_lon,)), dma((2 * n_lon,)),
            ],
            compiler_params=pltpu.CompilerParams(collective_id=0, has_side_effects=True),
        )(plan, velocity_start, forcing, strength, mobility, stress_in)
        return tuple(pl.pallas_call(
            hand_over,
            out_shape=tuple(jax.ShapeDtypeStruct(s, f32) for s in shapes),
            in_specs=[inside] * 3,
            out_specs=(pl.BlockSpec(memory_space=pltpu.HBM),) * 3,
            scratch_shapes=[dma((3,))],
            compiler_params=pltpu.CompilerParams(vmem_limit_bytes=1 << 20),
        )(*results))

    placed = (
        P(None, "lat", "lon"),
        P(None, "lat", "lon"),
        P("lat", "lon"),
        P("lat", "lon"),
        P("lat", "lon"),
        P("lat", "lon", None, None, None),
    )
    return jax.shard_map(
        body,
        mesh=mesh,
        in_specs=placed,
        out_specs=(P(None, "lat", "lon"), P(None, "lat", "lon"), P("lat", "lon", None, None, None)),
        check_vma=False,
    )
```

```python
import functools

import jax
import jax.numpy as jnp
from jax import lax
from jax.experimental import pallas as pl
from jax.experimental.pallas import tpu as pltpu
from jax.sharding import PartitionSpec as P

NSUB = 4
PARTS = 2
FAR_FIRST = (10, 9, 11, 6, 14, 5, 15, 7, 13, 2, 8, 1, 3, 4, 12)
DEPTH = 5
DECAY = 0.8
LANES = 128
HALO = 8
TOP = 16
MESH = pl.DeviceIdType.MESH
SPLIT = (pl.ds(2, 1), pl.ds(0, 2))


def kernel(
    n_lon, n_lat,
    plan_ref, vel_ref, frc_ref, str_ref, mob_ref, sig_ref,
    o_vel, o_frc, o_sig,
    cst, edge_l, edge_r, halo_r, halo_l,
    plan_own, plan_all, plan_sm, inv_own, inv_sm,
    part_a, part_b, pack, sig, uv, coef, inc, back_a, back_b, home,
    loc_sem, one_sem, first_sem, self_sem, p1_s, p1_r, pl_s, pl_r, x_s, x_r, y_s, y_r,
    p2_s, p2_r, h_s, h_r, r1_s, r1_r, r2_s, r2_r,
):
    me = lax.axis_index("lon")
    lat = lax.axis_index("lat")
    right, left = lax.rem(me + 1, n_lon), lax.rem(me + n_lon - 1, n_lon)
    below, above = lax.rem(lat + 1, n_lat), lax.rem(lat + n_lat - 1, n_lat)
    side = LANES
    all_cols = plan_ref.shape[1]
    cols = all_cols // PARTS
    slots = sig_ref.shape[1]
    piece = side // n_lon
    tiles = (side + 2 * HALO) // 8
    lane1 = lax.broadcasted_iota(jnp.int32, (1, LANES), 1)
    lane = lax.broadcasted_iota(jnp.int32, (1, 1, LANES), 2)

    def to(src, dst, ss, rs, **where):
        return pltpu.make_async_remote_copy(
            src_ref=src, dst_ref=dst, send_sem=ss, recv_sem=rs,
            device_id=where, device_id_type=MESH,
        )

    def each(fn):
        def step(k, carry):
            fn(lax.rem(me + k, n_lon))
            return carry
        lax.fori_loop(1, n_lon, step, 0)

    if n_lon == 16:
        y, x = lax.div(me, 4), lax.rem(me, 4)
        ahead = [4 * lax.rem(y + i // 4, 4) + lax.rem(x + i % 4, 4) for i in FAR_FIRST]
        behind = [4 * lax.rem(y + 4 - i // 4, 4) + lax.rem(x + 4 - i % 4, 4) for i in FAR_FIRST]
    else:
        ahead = [lax.rem(me + i, n_lon) for i in range(1, n_lon)]
        behind = [lax.rem(me + n_lon - i, n_lon) for i in range(1, n_lon)]

    def peers(fn, sign=1):
        for d in ahead if sign > 0 else behind:
            fn(d)

    def rows_of(d):
        return pl.ds(TOP + d * piece, piece)

    barrier = pltpu.get_barrier_semaphore()
    peers(lambda d: pl.semaphore_signal(barrier, inc=1, device_id={"lon": d}, device_id_type=MESH))
    for other in (above, below):
        pl.semaphore_signal(barrier, inc=1, device_id={"lat": other}, device_id_type=MESH)

    own_rows = pl.ds(TOP, side)
    copies = []
    for j in range(all_cols):
        h, t = divmod(j, cols)
        src_cols = pl.ds(j * LANES, LANES)
        copies += [
            (vel_ref.at[:, :, src_cols], cst.at[h, pl.ds(0, 2), t, own_rows, :]),
            (frc_ref.at[:, :, src_cols], cst.at[h, pl.ds(2, 2), t, own_rows, :]),
            (str_ref.at[:, src_cols], cst.at[h, 4, t, own_rows, :]),
            (mob_ref.at[:, src_cols], cst.at[h, 5, t, own_rows, :]),
        ]
    copies = [pltpu.make_async_copy(s, d, loc_sem.at[i]) for i, (s, d) in enumerate(copies)]
    for c in copies:
        c.start()
    row = jnp.full((1, LANES), -1, jnp.int32)
    for j in range(all_cols):
        h, t = divmod(j, cols)
        row = jnp.where(lane1 == j, plan_ref[0, j], row)
        active = jnp.where(plan_ref[0, j] >= 0, 1.0, 0.0)
        cst[h, 6, t, own_rows, :] = jnp.full((side, LANES), active, jnp.float32)
    plan_own[...] = row
    for c in copies:
        c.wait()

    to_left = jnp.zeros((side, LANES), jnp.float32)
    to_right = jnp.zeros((side, LANES), jnp.float32)
    for f in range(7):
        first, last = cst[0, f, 0, own_rows, :], cst[PARTS - 1, f, cols - 1, own_rows, :]
        if f:
            first = pltpu.roll(first, HALO * f, 1)
            last = pltpu.roll(last, LANES - HALO * f, 1)
        to_left = jnp.where((lane1 >= HALO * f) & (lane1 < HALO * (f + 1)), first, to_left)
        to_right = jnp.where(
            (lane1 >= LANES - HALO * (f + 1)) & (lane1 < LANES - HALO * f), last, to_right
        )
    half = side // 2
    low = lane1 < LANES // 2
    edge_l[...] = jnp.where(low, to_left[:half], pltpu.roll(to_left[half:], LANES // 2, 1))
    edge_r[...] = jnp.where(low, pltpu.roll(to_right[half:], LANES // 2, 1), to_right[:half])
    pl.semaphore_wait(barrier, n_lon + 1)

    part, back = (part_a, part_b), (back_a, back_b)

    def stage1(c, d, sender):
        fields = SPLIT[c]
        return to(
            sig_ref.at[0, :, fields, pl.ds(d * piece, piece), :],
            part[c].at[pl.ds(sender * slots, slots)],
            p1_s.at[c * n_lon + d], p1_r.at[c * n_lon + sender], lon=d,
        )

    def planmsg(d, sender):
        return to(plan_own, plan_all.at[sender], pl_s.at[d], pl_r.at[sender], lon=d)

    x_copies = [
        to(edge_l, halo_r, x_s.at[0], x_r.at[0], lon=left),
        to(edge_r, halo_l, x_s.at[1], x_r.at[1], lon=right),
    ]
    y_copies = []
    for i, span in enumerate((pl.ds(0, cols), pl.ds(cols, 1))):
        y_copies += [
            to(cst.at[:, :, span, pl.ds(TOP, HALO), :], cst.at[:, :, span, pl.ds(TOP + side, HALO), :],
               y_s.at[2 * i], y_r.at[2 * i], lat=above),
            to(cst.at[:, :, span, pl.ds(TOP + side - HALO, HALO), :],
               cst.at[:, :, span, pl.ds(TOP - HALO, HALO), :],
               y_s.at[2 * i + 1], y_r.at[2 * i + 1], lat=below),
        ]
    for c in x_copies:
        c.start()
    for c in y_copies[:2]:
        c.start()
    each(lambda d: planmsg(d, me).start())
    for c in range(2):
        peers(lambda d, c=c: stage1(c, d, me).start())
    self1 = [
        pltpu.make_async_copy(
            sig_ref.at[0, :, SPLIT[c], pl.ds(me * piece, piece), :],
            part[c].at[pl.ds(me * slots, slots)], first_sem.at[c],
        )
        for c in range(2)
    ]
    for c in self1:
        c.start()
    self_plan = pltpu.make_async_copy(plan_own, plan_all.at[me], one_sem.at[1])
    self_plan.start()

    each(lambda d: planmsg(d, d).wait_recv())
    self_plan.wait()
    plan_copy = pltpu.make_async_copy(plan_all, plan_sm, one_sem.at[2])
    plan_copy.start()
    plan_copy.wait()

    for c in self1:
        c.wait()

    def seat(c, d, j):
        return part[c][jnp.maximum(plan_sm[d, 0, j], 0)]

    def fill_first(h, d):
        for j in range(cols):
            pack[h, d, j] = seat(0, d, h * cols + j)[0]

    def fill_rest(h, d):
        for j in range(cols):
            block = seat(1, d, h * cols + j)
            pack[h, d, cols + j] = block[0]
            pack[h, d, 2 * cols + j] = block[1]
        if h:
            return
        both = jnp.zeros((piece, LANES), jnp.float32)
        for g in range(PARTS):
            after = (d, (g + 1) * cols) if g < PARTS - 1 else (lax.rem(d + 1, n_lon), 0)
            before = (d, g * cols - 1) if g else (lax.rem(d + n_lon - 1, n_lon), all_cols - 1)
            for f in range(3):
                i = 3 * g + f
                c, at = (1, f) if f < 2 else (0, 0)
                a, b = seat(c, *after)[at], seat(c, *before)[at]
                if i:
                    a, b = pltpu.roll(a, HALO * i, 1), pltpu.roll(b, LANES - HALO * i, 1)
                both = jnp.where((lane1 >= HALO * i) & (lane1 < HALO * (i + 1)), a, both)
                both = jnp.where((lane1 >= LANES - HALO * (i + 1)) & (lane1 < LANES - HALO * i), b, both)
        pack[0, d, 3 * cols] = both

    def width(h):
        return 3 * cols + (1 if h == 0 else 0)

    def stage2(h, c, d, sender):
        span = pl.ds(0, cols) if c == 0 else pl.ds(cols, width(h) - cols)
        slot = (2 * h + c) * n_lon
        if c == 0:
            return to(
                pack.at[:, d, span], sig.at[:, span, rows_of(sender), :],
                p2_s.at[d], p2_r.at[sender], lon=d,
            )
        return to(
            pack.at[h, d, span], sig.at[h, span, rows_of(sender), :],
            p2_s.at[slot + d], p2_r.at[slot + sender], lon=d,
        )

    def self2(h):
        span = pl.ds(0, width(h))
        return pltpu.make_async_copy(
            pack.at[h, me, span], sig.at[h, span, rows_of(me), :], self_sem.at[h]
        )

    def send_first(d):
        for h in range(PARTS):
            fill_first(h, d)
        stage2(0, 0, d, me).start()

    each(lambda d: stage1(0, d, d).wait_recv())
    peers(send_first)
    for h in range(PARTS):
        fill_first(h, me)
    for c in x_copies:
        c.wait_recv()
    for f in range(7):
        from_r, from_l = (
            jnp.concatenate([got[...], pltpu.roll(got[...], LANES // 2, 1)], 0) for got in (halo_r, halo_l)
        )
        if f:
            from_r = pltpu.roll(from_r, LANES - HALO * f, 1)
            from_l = pltpu.roll(from_l, HALO * f, 1)
        for h in range(PARTS):
            a = from_r if h == PARTS - 1 else cst[h + 1, f, 0, own_rows, :]
            b = from_l if h == 0 else cst[h - 1, f, cols - 1, own_rows, :]
            cst[h, f, cols, own_rows, :] = jnp.where(
                lane1 < HALO, a, jnp.where(lane1 >= LANES - HALO, b, 0.0)
            )
    for c in y_copies[2:]:
        c.start()

    each(lambda d: stage1(1, d, d).wait_recv())
    for h in range(PARTS):
        def send_rest(d, h=h):
            fill_rest(h, d)
            stage2(h, 1, d, me).start()
        peers(send_rest)
        fill_rest(h, me)
        self2(h).start()

    def invert(d, inv):
        for j in range(all_cols):
            inv = jnp.where(lane1 == plan_sm[d, 0, j], d * all_cols + j, inv)
        return inv
    inv_own[...] = lax.fori_loop(0, n_lon, invert, jnp.zeros((1, LANES), jnp.int32))
    inv_copy = pltpu.make_async_copy(inv_own, inv_sm, one_sem.at[3])
    inv_copy.start()

    def east(x):
        r = pltpu.roll(x, LANES - 1, 2)
        return jnp.where(lane == LANES - 1, jnp.concatenate([r[1:], r[:1]], 0), r)

    def west(x):
        r = pltpu.roll(x, 1, 2)
        return jnp.where(lane == 0, jnp.concatenate([r[-1:], r[:-1]], 0), r)

    def diff_x(x):
        return east(x) - west(x)

    def diff_y(ref, h, f, base):
        return ref[h, f, :, pl.ds(base + 1, 8), :] - ref[h, f, :, pl.ds(base - 1, 8), :]

    def increments(h, k, base, rows):
        u, v = uv[h, 0, :, rows, :], uv[h, 1, :, rows, :]
        ux, vx = diff_x(u), diff_x(v)
        uy, vy = diff_y(uv, h, 0, base), diff_y(uv, h, 1, base)
        div, ten, shr = ux + vy, ux - vy, uy + vx
        a = DECAY ** -k * coef[h, 0, :, rows, :]
        ar = a * lax.rsqrt(div * div + 0.25 * (ten * ten + shr * shr) + 0.25)
        ten4 = 0.25 * ten
        return ar * (div + ten4) - a, ar * (div - ten4) - a, ar * (0.25 * shr)

    def tile(t):
        base = pl.multiple_of(HALO + 8 * t, 8)
        return base, pl.ds(base, 8)

    def loop(lo, hi, fn, unroll=1):
        def step(t, carry):
            fn(*tile(t))
            return carry
        lax.fori_loop(lo, hi, step, 0, unroll=unroll)

    for c in y_copies:
        c.wait_recv()

    def prepare(h, t):
        base, rows = tile(t)
        outside = ((t == 0) & (lat == 0)) | ((t == tiles - 1) & (lat == n_lat - 1))
        mask = cst[h, 6, :, rows, :] * jnp.where(outside, 0.0, 1.0)
        mob = cst[h, 5, :, rows, :]
        ratio = mask / (5.0 + mob)
        push = ratio * mob
        sx, sy = cst[h, 0, :, rows, :], cst[h, 1, :, rows, :]
        uv[h, 0, :, rows, :] = mask * sx
        uv[h, 1, :, rows, :] = mask * sy
        coef[h, 0, :, rows, :] = 0.2 * mask * cst[h, 4, :, rows, :]
        coef[h, 1, :, rows, :] = 4.0 * ratio
        coef[h, 2, :, rows, :] = push
        coef[h, 3, :, rows, :] = ratio * sx + push * cst[h, 2, :, rows, :]
        coef[h, 4, :, rows, :] = ratio * sy + push * cst[h, 3, :, rows, :]
        coef[h, 5, :, rows, :] = mask

    def warm_up(h, carry):
        def step(t, inner):
            prepare(h, t)
            return inner
        lax.fori_loop(0, tiles, step, 0, unroll=6)

        def first(base, rows):
            for f, value in enumerate(increments(h, 1, base, rows)):
                inc[h, f, :, rows, :] = value
        loop(0, tiles, first, 6)
        return carry

    lax.fori_loop(0, PARTS, warm_up, 0)

    def stress_first(h, base, rows):
        w = coef[h, 5, :, rows, :]
        beside = sig[0, 3 * cols, rows, :]
        s = []
        for f in range(3):
            i, at = 3 * h + f, (1, 2, 0)[f] * cols
            extra = beside
            if i:
                extra = jnp.where(
                    lane1 < LANES // 2,
                    pltpu.roll(beside, LANES - HALO * i, 1), pltpu.roll(beside, HALO * i, 1),
                )
            s.append(jnp.concatenate([sig[h, pl.ds(at, cols), rows, :], extra[None]], 0))
        inc[h, 0, :, rows, :] += w * (s[0] + s[1])
        inc[h, 1, :, rows, :] += w * (s[0] - s[1])
        inc[h, 2, :, rows, :] += (w + w) * s[2]

    def stress_next(h, k, base, rows):
        for f, value in enumerate(increments(h, k, base, rows)):
            inc[h, f, :, rows, :] += value

    def momentum(h, k, base, rows, emit=False):
        scale = 0.25 * DECAY ** k
        fx = diff_x(inc[h, 0, :, rows, :]) + diff_y(inc, h, 2, base)
        fy = diff_x(inc[h, 2, :, rows, :]) + diff_y(inc, h, 1, base)
        u, v = uv[h, 0, :, rows, :], uv[h, 1, :, rows, :]
        keep, push = coef[h, 1, :, rows, :], scale * coef[h, 2, :, rows, :]
        turn = 0.3 / scale
        un = keep * u + coef[h, 3, :, rows, :] + push * (fx + turn * v)
        vn = keep * v + coef[h, 4, :, rows, :] + push * (fy - turn * u)
        if not emit:
            uv[h, 0, :, rows, :] = un
            uv[h, 1, :, rows, :] = vn
            return
        mask = scale * coef[h, 5, :, rows, :]
        fx, fy = mask * fx, mask * fy
        out_rows = pl.ds(pl.multiple_of(base - TOP, 8), 8)
        for j in range(cols):
            at = pl.ds(pl.multiple_of((h * cols + j) * LANES, LANES), LANES)
            o_vel[0, out_rows, at] = un[j]
            o_vel[1, out_rows, at] = vn[j]
            o_frc[0, out_rows, at] = fx[j]
            o_frc[1, out_rows, at] = fy[j]

    def take(h, sender):
        @pl.when(sender != me)
        def _():
            if h == 0:
                stage2(0, 0, sender, sender).wait_recv()
            stage2(h, 1, sender, sender).wait_recv()

        @pl.when(sender == me)
        def _():
            self2(h).wait()

    def piece_tiles(d, fn):
        for i in range(piece // 8):
            base = pl.multiple_of(TOP + d * piece + 8 * i, 8)
            fn(base, pl.ds(base, 8))

    def back1(h, c, d, sender):
        fields, slot = SPLIT[c], (2 * h + c) * n_lon
        return to(
            inc.at[h, fields, pl.ds(0, cols), rows_of(d), :], back[c].at[sender, h],
            r1_s.at[slot + d], r1_r.at[slot + sender], lon=d,
        )

    def self3(h, c):
        return pltpu.make_async_copy(
            inc.at[h, SPLIT[c], pl.ds(0, cols), rows_of(me), :], back[c].at[me, h],
            self_sem.at[PARTS + 2 * h + c],
        )

    def run(h):
        span = pl.ds(0, width(h))
        up = to(sig.at[h, span, pl.ds(TOP, HALO), :], sig.at[h, span, pl.ds(TOP + side, HALO), :],
                h_s.at[2 * h], h_r.at[2 * h], lat=above)
        down = to(sig.at[h, span, pl.ds(TOP + side - HALO, HALO), :],
                  sig.at[h, span, pl.ds(TOP - HALO, HALO), :],
                  h_s.at[2 * h + 1], h_r.at[2 * h + 1], lat=below)
        take(h, 0)
        up.start()
        take(h, n_lon - 1)
        down.start()
        first = functools.partial(stress_first, h)
        stages = []
        for k in range(1, NSUB):
            stages += [functools.partial(momentum, h, k), functools.partial(stress_next, h, k + 1)]

        def arrive(sender):
            @pl.when((sender != 0) & (sender != n_lon - 1))
            def _():
                take(h, sender)
            piece_tiles(sender, first)

        peers(arrive, -1)
        arrive(me)
        for i in range(DEPTH):
            loop(2 + i, tiles - 2 - i, stages[i], tiles - 4 - 2 * i)
        up.wait()
        down.wait()
        first(*tile(0))
        first(*tile(tiles - 1))
        for i, stage in enumerate(stages):
            if i < DEPTH:
                loop(0, 2 + i, stage, 2 + i)
                loop(tiles - 2 - i, tiles, stage, 2 + i)
            else:
                loop(0, tiles, stage, tiles)
        for c in range(2):
            peers(lambda d, c=c: back1(h, c, d, me).start())
        for c in range(2):
            self3(h, c).start()

    for h in range(PARTS):
        run(h)

    def finish(h, carry):
        loop(1, tiles - 1, functools.partial(momentum, h, NSUB, emit=True), 8)
        return carry

    lax.fori_loop(0, PARTS, finish, 0)

    def refill(c, d):
        for s in range(slots):
            block = inv_sm[0, d * slots + s]
            owner, column = lax.div(block, all_cols), lax.rem(block, all_cols)
            h, j = lax.div(column, cols), lax.rem(column, cols)
            scale = 0.5 * DECAY ** NSUB
            if c == 0:
                home[d, s, 2] = scale * back[0][owner, h, 0, j]
            if c == 1:
                plus, minus = scale * back[1][owner, h, 0, j], scale * back[1][owner, h, 1, j]
                home[d, s, 0] = plus + minus
                home[d, s, 1] = plus - minus

    def back2(c, d, sender):
        fields = SPLIT[c]
        return to(
            home.at[d, :, fields], o_sig.at[0, :, fields, pl.ds(sender * piece, piece), :],
            r2_s.at[c * n_lon + d], r2_r.at[c * n_lon + sender], lon=d,
        )

    inv_copy.wait()
    for h in range(PARTS):
        for c in range(2):
            self3(h, c).wait()
    for c in range(2):
        for h in range(PARTS):
            each(lambda d, h=h, c=c: back1(h, c, d, d).wait_recv())

        def send_back2(d, c=c):
            refill(c, d)
            back2(c, d, me).start()

        peers(send_back2)
        refill(c, me)
    self4 = pltpu.make_async_copy(
        home.at[me], o_sig.at[0, :, :, pl.ds(me * piece, piece), :], one_sem.at[4]
    )
    self4.start()

    for c in x_copies + y_copies:
        c.wait_send()

    def drain(d):
        planmsg(d, me).wait_send()
        stage2(0, 0, d, me).wait_send()
        for h in range(PARTS):
            stage2(h, 1, d, me).wait_send()
        for c in range(2):
            stage1(c, d, me).wait_send()
        for c in range(2):
            for h in range(PARTS):
                back1(h, c, d, me).wait_send()
            back2(c, d, me).wait_send()

    each(drain)
    self4.wait()
    for c in range(2):
        each(lambda d, c=c: back2(c, d, d).wait_recv())


def hand_over(*refs):
    sources, targets, sem = refs[:3], refs[3:6], refs[6]
    moves = [pltpu.make_async_copy(s, t, sem.at[i]) for i, (s, t) in enumerate(zip(sources, targets))]
    for m in moves:
        m.start()
    for m in moves:
        m.wait()


def solution(mesh):
    n_lon, n_lat = mesh.shape["lon"], mesh.shape["lat"]

    def body(velocity_start, forcing, strength, mobility, plan, stress_in):
        cols, slots, side = plan.shape[1], stress_in.shape[1], stress_in.shape[-1]
        cols = cols // PARTS
        piece, wide, tall = side // n_lon, cols + 1, side + 32
        f32, i32 = jnp.float32, jnp.int32
        vmem, dma = pltpu.VMEM, pltpu.SemaphoreType.DMA
        anywhere = pl.BlockSpec(memory_space=pl.ANY)
        inside = pl.BlockSpec(memory_space=pltpu.VMEM)
        shapes = (velocity_start.shape, forcing.shape, stress_in.shape)
        results = pl.pallas_call(
            functools.partial(kernel, n_lon, n_lat),
            out_shape=tuple(vmem(s, f32) for s in shapes),
            in_specs=[pl.BlockSpec(memory_space=pltpu.SMEM)] + [anywhere] * 5,
            out_specs=(inside,) * 3,
            scratch_shapes=[
                vmem((PARTS, 7, wide, tall, LANES), f32),
                vmem((side // 2, LANES), f32),
                vmem((side // 2, LANES), f32),
                vmem((side // 2, LANES), f32),
                vmem((side // 2, LANES), f32),
                vmem((1, LANES), i32),
                vmem((n_lon, 1, LANES), i32),
                pltpu.SMEM((n_lon, 1, LANES), i32),
                vmem((1, LANES), i32),
                pltpu.SMEM((1, LANES), i32),
                vmem((n_lon * slots, 1, piece, LANES), f32),
                vmem((n_lon * slots, 2, piece, LANES), f32),
                vmem((PARTS, n_lon, 3 * cols + 1, piece, LANES), f32),
                vmem((PARTS, 3 * cols + 1, tall, LANES), f32),
                vmem((PARTS, 2, wide, tall, LANES), f32),
                vmem((PARTS, 6, wide, tall, LANES), f32),
                vmem((PARTS, 3, wide, tall, LANES), f32),
                vmem((n_lon, PARTS, 1, cols, piece, LANES), f32),
                vmem((n_lon, PARTS, 2, cols, piece, LANES), f32),
                vmem((n_lon, slots, 3, piece, LANES), f32),
                dma((4 * cols * PARTS,)),
                dma((5,)),
                dma((2,)),
                dma((3 * PARTS,)),
                dma((2 * n_lon,)), dma((2 * n_lon,)),
                dma((n_lon,)), dma((n_lon,)),
                dma((2,)), dma((2,)),
                dma((4,)), dma((4,)),
                dma((2 * PARTS * n_lon,)), dma((2 * PARTS * n_lon,)),
                dma((2 * PARTS,)), dma((2 * PARTS,)),
                dma((2 * PARTS * n_lon,)), dma((2 * PARTS * n_lon,)),
                dma((2 * n_lon,)), dma((2 * n_lon,)),
            ],
            compiler_params=pltpu.CompilerParams(collective_id=0, has_side_effects=True),
        )(plan, velocity_start, forcing, strength, mobility, stress_in)
        return tuple(pl.pallas_call(
            hand_over,
            out_shape=tuple(jax.ShapeDtypeStruct(s, f32) for s in shapes),
            in_specs=[inside] * 3,
            out_specs=(pl.BlockSpec(memory_space=pltpu.HBM),) * 3,
            scratch_shapes=[dma((3,))],
            compiler_params=pltpu.CompilerParams(vmem_limit_bytes=1 << 20),
        )(*results))

    placed = (
        P(None, "lat", "lon"),
        P(None, "lat", "lon"),
        P("lat", "lon"),
        P("lat", "lon"),
        P("lat", "lon"),
        P("lat", "lon", None, None, None),
    )
    return jax.shard_map(
        body,
        mesh=mesh,
        in_specs=placed,
        out_specs=(P(None, "lat", "lon"), P(None, "lat", "lon"), P("lat", "lon", None, None, None)),
        check_vma=False,
    )
```

```python
import functools

import jax
import jax.numpy as jnp
from jax import lax
from jax.experimental import pallas as pl
from jax.experimental.pallas import tpu as pltpu
from jax.sharding import PartitionSpec as P

NSUB = 4
PARTS = 2
FAR_FIRST = (10, 9, 11, 6, 14, 5, 15, 7, 13, 2, 8, 1, 3, 4, 12)
DEPTH = 4
DECAY = 0.8
LANES = 128
HALO = 8
TOP = 16
MESH = pl.DeviceIdType.MESH
SPLIT = (pl.ds(2, 1), pl.ds(0, 2))


def kernel(
    n_lon, n_lat,
    plan_ref, vel_ref, frc_ref, str_ref, mob_ref, sig_ref,
    o_vel, o_frc, o_sig,
    cst, edge_l, edge_r, halo_r, halo_l,
    plan_own, plan_all, plan_sm, inv_own, inv_sm,
    part_a, part_b, pack, sig, uv, coef, inc, back_a, back_b, home,
    loc_sem, one_sem, first_sem, self_sem, p1_s, p1_r, pl_s, pl_r, x_s, x_r, y_s, y_r,
    p2_s, p2_r, h_s, h_r, r1_s, r1_r, r2_s, r2_r,
):
    me = lax.axis_index("lon")
    lat = lax.axis_index("lat")
    right, left = lax.rem(me + 1, n_lon), lax.rem(me + n_lon - 1, n_lon)
    below, above = lax.rem(lat + 1, n_lat), lax.rem(lat + n_lat - 1, n_lat)
    side = LANES
    all_cols = plan_ref.shape[1]
    cols = all_cols // PARTS
    slots = sig_ref.shape[1]
    piece = side // n_lon
    tiles = (side + 2 * HALO) // 8
    lane1 = lax.broadcasted_iota(jnp.int32, (1, LANES), 1)
    lane = lax.broadcasted_iota(jnp.int32, (1, 1, LANES), 2)

    def to(src, dst, ss, rs, **where):
        return pltpu.make_async_remote_copy(
            src_ref=src, dst_ref=dst, send_sem=ss, recv_sem=rs,
            device_id=where, device_id_type=MESH,
        )

    def each(fn):
        def step(k, carry):
            fn(lax.rem(me + k, n_lon))
            return carry
        lax.fori_loop(1, n_lon, step, 0)

    if n_lon == 16:
        y, x = lax.div(me, 4), lax.rem(me, 4)
        ahead = [4 * lax.rem(y + i // 4, 4) + lax.rem(x + i % 4, 4) for i in FAR_FIRST]
        behind = [4 * lax.rem(y + 4 - i // 4, 4) + lax.rem(x + 4 - i % 4, 4) for i in FAR_FIRST]
    else:
        ahead = [lax.rem(me + i, n_lon) for i in range(1, n_lon)]
        behind = [lax.rem(me + n_lon - i, n_lon) for i in range(1, n_lon)]

    def peers(fn, sign=1):
        for d in ahead if sign > 0 else behind:
            fn(d)

    def rows_of(d):
        return pl.ds(TOP + d * piece, piece)

    barrier = pltpu.get_barrier_semaphore()
    peers(lambda d: pl.semaphore_signal(barrier, inc=1, device_id={"lon": d}, device_id_type=MESH))
    for other in (above, below):
        pl.semaphore_signal(barrier, inc=1, device_id={"lat": other}, device_id_type=MESH)

    own_rows = pl.ds(TOP, side)
    copies = []
    for j in range(all_cols):
        h, t = divmod(j, cols)
        src_cols = pl.ds(j * LANES, LANES)
        copies += [
            (vel_ref.at[:, :, src_cols], cst.at[h, pl.ds(0, 2), t, own_rows, :]),
            (frc_ref.at[:, :, src_cols], cst.at[h, pl.ds(2, 2), t, own_rows, :]),
            (str_ref.at[:, src_cols], cst.at[h, 4, t, own_rows, :]),
            (mob_ref.at[:, src_cols], cst.at[h, 5, t, own_rows, :]),
        ]
    copies = [pltpu.make_async_copy(s, d, loc_sem.at[i]) for i, (s, d) in enumerate(copies)]
    for c in copies:
        c.start()
    row = jnp.full((1, LANES), -1, jnp.int32)
    for j in range(all_cols):
        h, t = divmod(j, cols)
        row = jnp.where(lane1 == j, plan_ref[0, j], row)
        active = jnp.where(plan_ref[0, j] >= 0, 1.0, 0.0)
        cst[h, 6, t, own_rows, :] = jnp.full((side, LANES), active, jnp.float32)
    plan_own[...] = row
    for c in copies:
        c.wait()

    to_left = jnp.zeros((side, LANES), jnp.float32)
    to_right = jnp.zeros((side, LANES), jnp.float32)
    for f in range(7):
        first, last = cst[0, f, 0, own_rows, :], cst[PARTS - 1, f, cols - 1, own_rows, :]
        if f:
            first = pltpu.roll(first, HALO * f, 1)
            last = pltpu.roll(last, LANES - HALO * f, 1)
        to_left = jnp.where((lane1 >= HALO * f) & (lane1 < HALO * (f + 1)), first, to_left)
        to_right = jnp.where(
            (lane1 >= LANES - HALO * (f + 1)) & (lane1 < LANES - HALO * f), last, to_right
        )
    half = side // 2
    low = lane1 < LANES // 2
    edge_l[...] = jnp.where(low, to_left[:half], pltpu.roll(to_left[half:], LANES // 2, 1))
    edge_r[...] = jnp.where(low, pltpu.roll(to_right[half:], LANES // 2, 1), to_right[:half])
    pl.semaphore_wait(barrier, n_lon + 1)

    part, back = (part_a, part_b), (back_a, back_b)

    def stage1(c, d, sender):
        fields = SPLIT[c]
        return to(
            sig_ref.at[0, :, fields, pl.ds(d * piece, piece), :],
            part[c].at[pl.ds(sender * slots, slots)],
            p1_s.at[c * n_lon + d], p1_r.at[c * n_lon + sender], lon=d,
        )

    def planmsg(d, sender):
        return to(plan_own, plan_all.at[sender], pl_s.at[d], pl_r.at[sender], lon=d)

    x_copies = [
        to(edge_l, halo_r, x_s.at[0], x_r.at[0], lon=left),
        to(edge_r, halo_l, x_s.at[1], x_r.at[1], lon=right),
    ]
    y_copies = []
    for i, span in enumerate((pl.ds(0, cols), pl.ds(cols, 1))):
        y_copies += [
            to(cst.at[:, :, span, pl.ds(TOP, HALO), :], cst.at[:, :, span, pl.ds(TOP + side, HALO), :],
               y_s.at[2 * i], y_r.at[2 * i], lat=above),
            to(cst.at[:, :, span, pl.ds(TOP + side - HALO, HALO), :],
               cst.at[:, :, span, pl.ds(TOP - HALO, HALO), :],
               y_s.at[2 * i + 1], y_r.at[2 * i + 1], lat=below),
        ]
    for c in x_copies:
        c.start()
    for c in y_copies[:2]:
        c.start()
    each(lambda d: planmsg(d, me).start())
    for c in range(2):
        peers(lambda d, c=c: stage1(c, d, me).start())
    self1 = [
        pltpu.make_async_copy(
            sig_ref.at[0, :, SPLIT[c], pl.ds(me * piece, piece), :],
            part[c].at[pl.ds(me * slots, slots)], first_sem.at[c],
        )
        for c in range(2)
    ]
    for c in self1:
        c.start()
    self_plan = pltpu.make_async_copy(plan_own, plan_all.at[me], one_sem.at[1])
    self_plan.start()

    each(lambda d: planmsg(d, d).wait_recv())
    self_plan.wait()
    plan_copy = pltpu.make_async_copy(plan_all, plan_sm, one_sem.at[2])
    plan_copy.start()
    plan_copy.wait()

    for c in self1:
        c.wait()

    def seat(c, d, j):
        return part[c][jnp.maximum(plan_sm[d, 0, j], 0)]

    def fill_first(h, d):
        for j in range(cols):
            pack[h, d, j] = seat(0, d, h * cols + j)[0]

    def fill_rest(h, d):
        for j in range(cols):
            block = seat(1, d, h * cols + j)
            pack[h, d, cols + j] = block[0]
            pack[h, d, 2 * cols + j] = block[1]
        if h:
            return
        both = jnp.zeros((piece, LANES), jnp.float32)
        for g in range(PARTS):
            after = (d, (g + 1) * cols) if g < PARTS - 1 else (lax.rem(d + 1, n_lon), 0)
            before = (d, g * cols - 1) if g else (lax.rem(d + n_lon - 1, n_lon), all_cols - 1)
            for f in range(3):
                i = 3 * g + f
                c, at = (1, f) if f < 2 else (0, 0)
                a, b = seat(c, *after)[at], seat(c, *before)[at]
                if i:
                    a, b = pltpu.roll(a, HALO * i, 1), pltpu.roll(b, LANES - HALO * i, 1)
                both = jnp.where((lane1 >= HALO * i) & (lane1 < HALO * (i + 1)), a, both)
                both = jnp.where((lane1 >= LANES - HALO * (i + 1)) & (lane1 < LANES - HALO * i), b, both)
        pack[0, d, 3 * cols] = both

    def width(h):
        return 3 * cols + (1 if h == 0 else 0)

    def stage2(h, c, d, sender):
        span = pl.ds(0, cols) if c == 0 else pl.ds(cols, width(h) - cols)
        slot = (2 * h + c) * n_lon
        if c == 0:
            return to(
                pack.at[:, d, span], sig.at[:, span, rows_of(sender), :],
                p2_s.at[d], p2_r.at[sender], lon=d,
            )
        return to(
            pack.at[h, d, span], sig.at[h, span, rows_of(sender), :],
            p2_s.at[slot + d], p2_r.at[slot + sender], lon=d,
        )

    def self2(h):
        span = pl.ds(0, width(h))
        return pltpu.make_async_copy(
            pack.at[h, me, span], sig.at[h, span, rows_of(me), :], self_sem.at[h]
        )

    def send_first(d):
        for h in range(PARTS):
            fill_first(h, d)
        stage2(0, 0, d, me).start()

    each(lambda d: stage1(0, d, d).wait_recv())
    peers(send_first)
    for h in range(PARTS):
        fill_first(h, me)
    for c in x_copies:
        c.wait_recv()
    for f in range(7):
        from_r, from_l = (
            jnp.concatenate([got[...], pltpu.roll(got[...], LANES // 2, 1)], 0) for got in (halo_r, halo_l)
        )
        if f:
            from_r = pltpu.roll(from_r, LANES - HALO * f, 1)
            from_l = pltpu.roll(from_l, HALO * f, 1)
        for h in range(PARTS):
            a = from_r if h == PARTS - 1 else cst[h + 1, f, 0, own_rows, :]
            b = from_l if h == 0 else cst[h - 1, f, cols - 1, own_rows, :]
            cst[h, f, cols, own_rows, :] = jnp.where(
                lane1 < HALO, a, jnp.where(lane1 >= LANES - HALO, b, 0.0)
            )
    for c in y_copies[2:]:
        c.start()

    each(lambda d: stage1(1, d, d).wait_recv())
    for h in range(PARTS):
        def send_rest(d, h=h):
            fill_rest(h, d)
            stage2(h, 1, d, me).start()
        peers(send_rest)
        fill_rest(h, me)
        self2(h).start()

    def invert(d, inv):
        for j in range(all_cols):
            inv = jnp.where(lane1 == plan_sm[d, 0, j], d * all_cols + j, inv)
        return inv
    inv_own[...] = lax.fori_loop(0, n_lon, invert, jnp.zeros((1, LANES), jnp.int32))
    inv_copy = pltpu.make_async_copy(inv_own, inv_sm, one_sem.at[3])
    inv_copy.start()

    def east(x):
        r = pltpu.roll(x, LANES - 1, 2)
        return jnp.where(lane == LANES - 1, jnp.concatenate([r[1:], r[:1]], 0), r)

    def west(x):
        r = pltpu.roll(x, 1, 2)
        return jnp.where(lane == 0, jnp.concatenate([r[-1:], r[:-1]], 0), r)

    def diff_x(x):
        return east(x) - west(x)

    def diff_y(ref, h, f, base):
        return ref[h, f, :, pl.ds(base + 1, 8), :] - ref[h, f, :, pl.ds(base - 1, 8), :]

    def increments(h, k, base, rows):
        u, v = uv[h, 0, :, rows, :], uv[h, 1, :, rows, :]
        ux, vx = diff_x(u), diff_x(v)
        uy, vy = diff_y(uv, h, 0, base), diff_y(uv, h, 1, base)
        div, ten, shr = ux + vy, ux - vy, uy + vx
        a = DECAY ** -k * coef[h, 0, :, rows, :]
        ar = a * lax.rsqrt(div * div + 0.25 * (ten * ten + shr * shr) + 0.25)
        ten4 = 0.25 * ten
        return ar * (div + ten4) - a, ar * (div - ten4) - a, ar * (0.25 * shr)

    def tile(t):
        base = pl.multiple_of(HALO + 8 * t, 8)
        return base, pl.ds(base, 8)

    def loop(lo, hi, fn, unroll=1):
        def step(t, carry):
            fn(*tile(t))
            return carry
        lax.fori_loop(lo, hi, step, 0, unroll=unroll)

    for c in y_copies:
        c.wait_recv()

    def prepare(h, t):
        base, rows = tile(t)
        outside = ((t == 0) & (lat == 0)) | ((t == tiles - 1) & (lat == n_lat - 1))
        mask = cst[h, 6, :, rows, :] * jnp.where(outside, 0.0, 1.0)
        mob = cst[h, 5, :, rows, :]
        ratio = mask / (5.0 + mob)
        push = ratio * mob
        sx, sy = cst[h, 0, :, rows, :], cst[h, 1, :, rows, :]
        uv[h, 0, :, rows, :] = mask * sx
        uv[h, 1, :, rows, :] = mask * sy
        coef[h, 0, :, rows, :] = 0.2 * mask * cst[h, 4, :, rows, :]
        coef[h, 1, :, rows, :] = 4.0 * ratio
        coef[h, 2, :, rows, :] = push
        coef[h, 3, :, rows, :] = ratio * sx + push * cst[h, 2, :, rows, :]
        coef[h, 4, :, rows, :] = ratio * sy + push * cst[h, 3, :, rows, :]
        coef[h, 5, :, rows, :] = mask

    def warm_up(h, carry):
        def step(t, inner):
            prepare(h, t)
            return inner
        lax.fori_loop(0, tiles, step, 0, unroll=6)

        def first(base, rows):
            for f, value in enumerate(increments(h, 1, base, rows)):
                inc[h, f, :, rows, :] = value
        loop(0, tiles, first, 6)
        return carry

    lax.fori_loop(0, PARTS, warm_up, 0)

    def stress_first(h, base, rows):
        w = coef[h, 5, :, rows, :]
        beside = sig[0, 3 * cols, rows, :]
        s = []
        for f in range(3):
            i, at = 3 * h + f, (1, 2, 0)[f] * cols
            extra = beside
            if i:
                extra = jnp.where(
                    lane1 < LANES // 2,
                    pltpu.roll(beside, LANES - HALO * i, 1), pltpu.roll(beside, HALO * i, 1),
                )
            s.append(jnp.concatenate([sig[h, pl.ds(at, cols), rows, :], extra[None]], 0))
        inc[h, 0, :, rows, :] += w * (s[0] + s[1])
        inc[h, 1, :, rows, :] += w * (s[0] - s[1])
        inc[h, 2, :, rows, :] += (w + w) * s[2]

    def stress_next(h, k, base, rows):
        for f, value in enumerate(increments(h, k, base, rows)):
            inc[h, f, :, rows, :] += value

    def momentum(h, k, base, rows, emit=False):
        scale = 0.25 * DECAY ** k
        fx = diff_x(inc[h, 0, :, rows, :]) + diff_y(inc, h, 2, base)
        fy = diff_x(inc[h, 2, :, rows, :]) + diff_y(inc, h, 1, base)
        u, v = uv[h, 0, :, rows, :], uv[h, 1, :, rows, :]
        keep, push = coef[h, 1, :, rows, :], scale * coef[h, 2, :, rows, :]
        turn = 0.3 / scale
        un = keep * u + coef[h, 3, :, rows, :] + push * (fx + turn * v)
        vn = keep * v + coef[h, 4, :, rows, :] + push * (fy - turn * u)
        if not emit:
            uv[h, 0, :, rows, :] = un
            uv[h, 1, :, rows, :] = vn
            return
        mask = scale * coef[h, 5, :, rows, :]
        fx, fy = mask * fx, mask * fy
        out_rows = pl.ds(pl.multiple_of(base - TOP, 8), 8)
        for j in range(cols):
            at = pl.ds(pl.multiple_of((h * cols + j) * LANES, LANES), LANES)
            o_vel[0, out_rows, at] = un[j]
            o_vel[1, out_rows, at] = vn[j]
            o_frc[0, out_rows, at] = fx[j]
            o_frc[1, out_rows, at] = fy[j]

    def take(h, sender):
        @pl.when(sender != me)
        def _():
            if h == 0:
                stage2(0, 0, sender, sender).wait_recv()
            stage2(h, 1, sender, sender).wait_recv()

        @pl.when(sender == me)
        def _():
            self2(h).wait()

    def piece_tiles(d, fn):
        for i in range(piece // 8):
            base = pl.multiple_of(TOP + d * piece + 8 * i, 8)
            fn(base, pl.ds(base, 8))

    def back1(h, c, d, sender):
        fields, slot = SPLIT[c], (2 * h + c) * n_lon
        return to(
            inc.at[h, fields, pl.ds(0, cols), rows_of(d), :], back[c].at[sender, h],
            r1_s.at[slot + d], r1_r.at[slot + sender], lon=d,
        )

    def self3(h, c):
        return pltpu.make_async_copy(
            inc.at[h, SPLIT[c], pl.ds(0, cols), rows_of(me), :], back[c].at[me, h],
            self_sem.at[PARTS + 2 * h + c],
        )

    def run(h):
        span = pl.ds(0, width(h))
        up = to(sig.at[h, span, pl.ds(TOP, HALO), :], sig.at[h, span, pl.ds(TOP + side, HALO), :],
                h_s.at[2 * h], h_r.at[2 * h], lat=above)
        down = to(sig.at[h, span, pl.ds(TOP + side - HALO, HALO), :],
                  sig.at[h, span, pl.ds(TOP - HALO, HALO), :],
                  h_s.at[2 * h + 1], h_r.at[2 * h + 1], lat=below)
        take(h, 0)
        up.start()
        take(h, n_lon - 1)
        down.start()
        first = functools.partial(stress_first, h)
        stages = []
        for k in range(1, NSUB):
            stages += [functools.partial(momentum, h, k), functools.partial(stress_next, h, k + 1)]

        def arrive(sender):
            @pl.when((sender != 0) & (sender != n_lon - 1))
            def _():
                take(h, sender)
            piece_tiles(sender, first)

        peers(arrive, -1)
        arrive(me)
        for i in range(DEPTH):
            loop(2 + i, tiles - 2 - i, stages[i], tiles - 4 - 2 * i)
        up.wait()
        down.wait()
        first(*tile(0))
        first(*tile(tiles - 1))
        for i, stage in enumerate(stages):
            if i < DEPTH:
                loop(0, 2 + i, stage, 2 + i)
                loop(tiles - 2 - i, tiles, stage, 2 + i)
            else:
                loop(0, tiles, stage, tiles)
        for c in range(2):
            peers(lambda d, c=c: back1(h, c, d, me).start())
        for c in range(2):
            self3(h, c).start()

    for h in range(PARTS):
        run(h)

    def finish(h, carry):
        loop(1, tiles - 1, functools.partial(momentum, h, NSUB, emit=True), 8)
        return carry

    lax.fori_loop(0, PARTS, finish, 0)

    def refill(c, d):
        for s in range(slots):
            block = inv_sm[0, d * slots + s]
            owner, column = lax.div(block, all_cols), lax.rem(block, all_cols)
            h, j = lax.div(column, cols), lax.rem(column, cols)
            scale = 0.5 * DECAY ** NSUB
            if c == 0:
                home[d, s, 2] = scale * back[0][owner, h, 0, j]
            if c == 1:
                plus, minus = scale * back[1][owner, h, 0, j], scale * back[1][owner, h, 1, j]
                home[d, s, 0] = plus + minus
                home[d, s, 1] = plus - minus

    def back2(c, d, sender):
        fields = SPLIT[c]
        return to(
            home.at[d, :, fields], o_sig.at[0, :, fields, pl.ds(sender * piece, piece), :],
            r2_s.at[c * n_lon + d], r2_r.at[c * n_lon + sender], lon=d,
        )

    inv_copy.wait()
    for h in range(PARTS):
        for c in range(2):
            self3(h, c).wait()
    for c in range(2):
        for h in range(PARTS):
            each(lambda d, h=h, c=c: back1(h, c, d, d).wait_recv())

        def send_back2(d, c=c):
            refill(c, d)
            back2(c, d, me).start()

        peers(send_back2)
        refill(c, me)
    self4 = pltpu.make_async_copy(
        home.at[me], o_sig.at[0, :, :, pl.ds(me * piece, piece), :], one_sem.at[4]
    )
    self4.start()

    for c in x_copies + y_copies:
        c.wait_send()

    def drain(d):
        planmsg(d, me).wait_send()
        stage2(0, 0, d, me).wait_send()
        for h in range(PARTS):
            stage2(h, 1, d, me).wait_send()
        for c in range(2):
            stage1(c, d, me).wait_send()
        for c in range(2):
            for h in range(PARTS):
                back1(h, c, d, me).wait_send()
            back2(c, d, me).wait_send()

    each(drain)
    self4.wait()
    for c in range(2):
        each(lambda d, c=c: back2(c, d, d).wait_recv())


def hand_over(*refs):
    sources, targets, sem = refs[:3], refs[3:6], refs[6]
    moves = [pltpu.make_async_copy(s, t, sem.at[i]) for i, (s, t) in enumerate(zip(sources, targets))]
    for m in moves:
        m.start()
    for m in moves:
        m.wait()


def solution(mesh):
    n_lon, n_lat = mesh.shape["lon"], mesh.shape["lat"]

    def body(velocity_start, forcing, strength, mobility, plan, stress_in):
        cols, slots, side = plan.shape[1], stress_in.shape[1], stress_in.shape[-1]
        cols = cols // PARTS
        piece, wide, tall = side // n_lon, cols + 1, side + 32
        f32, i32 = jnp.float32, jnp.int32
        vmem, dma = pltpu.VMEM, pltpu.SemaphoreType.DMA
        anywhere = pl.BlockSpec(memory_space=pl.ANY)
        inside = pl.BlockSpec(memory_space=pltpu.VMEM)
        shapes = (velocity_start.shape, forcing.shape, stress_in.shape)
        results = pl.pallas_call(
            functools.partial(kernel, n_lon, n_lat),
            out_shape=tuple(vmem(s, f32) for s in shapes),
            in_specs=[pl.BlockSpec(memory_space=pltpu.SMEM)] + [anywhere] * 5,
            out_specs=(inside,) * 3,
            scratch_shapes=[
                vmem((PARTS, 7, wide, tall, LANES), f32),
                vmem((side // 2, LANES), f32),
                vmem((side // 2, LANES), f32),
                vmem((side // 2, LANES), f32),
                vmem((side // 2, LANES), f32),
                vmem((1, LANES), i32),
                vmem((n_lon, 1, LANES), i32),
                pltpu.SMEM((n_lon, 1, LANES), i32),
                vmem((1, LANES), i32),
                pltpu.SMEM((1, LANES), i32),
                vmem((n_lon * slots, 1, piece, LANES), f32),
                vmem((n_lon * slots, 2, piece, LANES), f32),
                vmem((PARTS, n_lon, 3 * cols + 1, piece, LANES), f32),
                vmem((PARTS, 3 * cols + 1, tall, LANES), f32),
                vmem((PARTS, 2, wide, tall, LANES), f32),
                vmem((PARTS, 6, wide, tall, LANES), f32),
                vmem((PARTS, 3, wide, tall, LANES), f32),
                vmem((n_lon, PARTS, 1, cols, piece, LANES), f32),
                vmem((n_lon, PARTS, 2, cols, piece, LANES), f32),
                vmem((n_lon, slots, 3, piece, LANES), f32),
                dma((4 * cols * PARTS,)),
                dma((5,)),
                dma((2,)),
                dma((3 * PARTS,)),
                dma((2 * n_lon,)), dma((2 * n_lon,)),
                dma((n_lon,)), dma((n_lon,)),
                dma((2,)), dma((2,)),
                dma((4,)), dma((4,)),
                dma((2 * PARTS * n_lon,)), dma((2 * PARTS * n_lon,)),
                dma((2 * PARTS,)), dma((2 * PARTS,)),
                dma((2 * PARTS * n_lon,)), dma((2 * PARTS * n_lon,)),
                dma((2 * n_lon,)), dma((2 * n_lon,)),
            ],
            compiler_params=pltpu.CompilerParams(collective_id=0, has_side_effects=True),
        )(plan, velocity_start, forcing, strength, mobility, stress_in)
        return tuple(pl.pallas_call(
            hand_over,
            out_shape=tuple(jax.ShapeDtypeStruct(s, f32) for s in shapes),
            in_specs=[inside] * 3,
            out_specs=(pl.BlockSpec(memory_space=pltpu.HBM),) * 3,
            scratch_shapes=[dma((3,))],
            compiler_params=pltpu.CompilerParams(vmem_limit_bytes=1 << 20),
        )(*results))

    placed = (
        P(None, "lat", "lon"),
        P(None, "lat", "lon"),
        P("lat", "lon"),
        P("lat", "lon"),
        P("lat", "lon"),
        P("lat", "lon", None, None, None),
    )
    return jax.shard_map(
        body,
        mesh=mesh,
        in_specs=placed,
        out_specs=(P(None, "lat", "lon"), P(None, "lat", "lon"), P("lat", "lon", None, None, None)),
        check_vma=False,
    )
```
